128 devices in a mesh: ctx: 4 (over z_hi, core), fsdp: 32 (over z_lo, x, y).
Axes of the slice: x: 4, y: 4, z: 4 (z_hi: 2, z_lo: 2; z = z_hi * 2 + z_lo), core: 2. Of those that a mesh axis runs over, the one named last changes fastest.
Arguments:
- query: bfloat16 [2, 8192, 4096], P(None, ('ctx', 'fsdp')), may hold values from -64 to 64
- key: bfloat16 [2, 8192, 2048], P(None, ('ctx', 'fsdp')), may hold values from -32 to 32
- value: bfloat16 [2, 8192, 2048], P(None, ('ctx', 'fsdp')), may hold values from -6 to 6
- grad_out: bfloat16 [2, 8192, 4096], P(None, ('ctx', 'fsdp')), may hold values from -6 to 6
- tile_start: int32 [2, 64], replicated, may hold values from 0 to 63, as said below
Outputs:
- grad_query: bfloat16 [2, 8192, 4096], P(None, ('ctx', 'fsdp'))
- grad_key: bfloat16 [2, 8192, 2048], P(None, ('ctx', 'fsdp'))
- grad_value: bfloat16 [2, 8192, 2048], P(None, ('ctx', 'fsdp'))
The draws below stay inside these ranges and needn't reach their ends.
Inputs may be any that keep to these rules, and one draw needn't show every extreme that they name: tile_start[b, t] is the first tile of the document holding tile t: it equals t or tile_start[b, t - 1], and tile_start[b, 0] = 0; the last tile of every sequence begins a document; no document begins at a tile whose first token is a nonzero multiple of 2048.
All inputs are finite; a program needn't handle non-finite values.
Results may differ from the reference program's by a relative error of at most 0.012.
Values may be sent and summed in bfloat16 or wider, within the bound.
A program may use at most 64 MiB of HBM per device.

```python
import jax
import jax.numpy as jnp
from jax import lax

HEADS = 32
KV_HEADS = 16
HEAD_DIM = 128
WINDOW = 1024
SEQ_LEN = 8192
TILE = 128
QBLOCK = 512
SEQS = 2
BLOCK_LEN = 2048


def shared_keys(key):
    shape = (SEQS, SEQ_LEN, KV_HEADS, HEAD_DIM)
    base = jnp.clip(jax.random.normal(jax.random.fold_in(key, 101), shape, jnp.float32), -6.0, 6.0)
    return base


def draw_key(key, part):
    return shared_keys(key).reshape(SEQS, SEQ_LEN, KV_HEADS * HEAD_DIM).astype(jnp.bfloat16)


def draw_query(key, part):
    shape = (SEQS, SEQ_LEN, HEADS, HEAD_DIM)
    base = jnp.clip(jax.random.normal(jax.random.fold_in(key, 201), shape, jnp.float32), -6.0, 6.0)
    return base.reshape(SEQS, SEQ_LEN, HEADS * HEAD_DIM).astype(jnp.bfloat16)


def draw_tile_start(key, part):
    tiles = SEQ_LEN // TILE
    levels = jax.random.randint(jax.random.fold_in(key, 301), (SEQS, 8), 0, 4)
    table = jnp.array([0, 1, 4, 12], jnp.int32)
    limits = jnp.sum(jnp.where(levels[:, :, None] == jnp.arange(4)[None, None, :], table[None, None, :], 0), axis=2)
    limits = jnp.repeat(limits, tiles // 8, axis=1)
    rolls = jax.random.randint(jax.random.fold_in(key, 302), (SEQS, tiles), 0, 16)
    place = jnp.arange(tiles, dtype=jnp.int32)[None, :]
    begins = (rolls < limits) & (place % (BLOCK_LEN // TILE) != 0)
    begins = begins | (place == 0) | (place == tiles - 1)
    marks = jnp.where(begins, place, 0).astype(jnp.int32)
    return lax.cummax(marks, axis=1)


def level_of(key, extent, shards, low, largest):
    gain = 1.0
    for position, blocks in shards:
        draws = jax.random.uniform(jax.random.fold_in(jax.random.fold_in(key, 6), position), (blocks,), jnp.float32, low / len(shards), largest / len(shards))
        gain = gain * jnp.repeat(jnp.exp(draws), extent[position] // blocks).reshape((-1,) + (1,) * (len(extent) - 1 - position))
    return gain


def noise(stream_key, extent, width, most, split=(), held_as=jnp.bfloat16):
    values = jax.random.normal(stream_key, extent, jnp.float32) * width
    if len(split) > 0:
        values = level_of(stream_key, extent, split, -0.22, 0.18) * values
    return jnp.clip(values, min=-most, max=most).astype(held_as)


def setup_inputs(seed: int = 0) -> dict:
    key_of = jax.random.split(jax.random.key(seed), 6)
    query = draw_query(jax.random.fold_in(key_of[5], 71), 0)
    key = draw_key(jax.random.fold_in(key_of[5], 71), 0)
    value = noise(key_of[2], (SEQS, SEQ_LEN, KV_HEADS * HEAD_DIM), 1.0, 6.0, ((1, 128),))
    grad_out = noise(key_of[3], (SEQS, SEQ_LEN, HEADS * HEAD_DIM), 1.0, 6.0, ((1, 128),))
    tile_start = draw_tile_start(jax.random.fold_in(key_of[5], 71), 0)
    return {"query": query, "key": key, "value": value, "grad_out": grad_out, "tile_start": tile_start}


score_scale = 168.0 ** -0.5


def block_grads(q_blk, g_blk, k_span, v_span, visible):
    hi = lax.Precision.HIGHEST
    qf = q_blk.astype(jnp.float32)
    gf = g_blk.astype(jnp.float32)
    kf = k_span.astype(jnp.float32)
    vf = v_span.astype(jnp.float32)
    scores = jnp.einsum("qhd,khd->hqk", qf, kf, precision=hi) * score_scale
    top = jnp.max(jnp.where(visible, scores, -jnp.inf), axis=-1, keepdims=True)
    weights = jnp.exp(jnp.where(visible, scores - top, -jnp.inf))
    probs = weights / jnp.sum(weights, axis=-1, keepdims=True)
    probs_low = probs.astype(jnp.bfloat16)
    grad_probs = jnp.einsum("qhd,khd->hqk", gf, vf, precision=hi)
    delta = jnp.sum(probs * grad_probs, axis=-1, keepdims=True)
    grad_scores = (probs * (grad_probs - delta)).astype(jnp.bfloat16)
    gsf = grad_scores.astype(jnp.float32)
    grad_q = (jnp.einsum("hqk,khd->qhd", gsf, kf, precision=hi) * score_scale).astype(jnp.bfloat16)
    grad_k = jnp.einsum("hqk,qhd->khd", gsf, qf, precision=hi) * score_scale
    grad_v = jnp.einsum("hqk,qhd->khd", probs_low.astype(jnp.float32), gf, precision=hi)
    return grad_q, grad_k, grad_v


def one_sequence(query, key, value, grad_out, tiles):
    span = QBLOCK + WINDOW
    q_all = query.reshape(SEQ_LEN, HEADS, HEAD_DIM)
    g_all = grad_out.reshape(SEQ_LEN, HEADS, HEAD_DIM)
    k_all = jnp.repeat(key.reshape(SEQ_LEN, KV_HEADS, HEAD_DIM), 2, axis=1)
    v_all = jnp.repeat(value.reshape(SEQ_LEN, KV_HEADS, HEAD_DIM), 2, axis=1)
    padding = jnp.zeros((WINDOW, HEADS, HEAD_DIM), k_all.dtype)
    k_ext = jnp.concatenate([padding, k_all], axis=0)
    v_ext = jnp.concatenate([padding, v_all], axis=0)
    starts = TILE * jnp.repeat(tiles, TILE)

    def step(index, carry):
        grad_q, grad_k, grad_v = carry
        q0 = jnp.asarray(index, jnp.int32) * QBLOCK
        q_blk = lax.dynamic_slice_in_dim(q_all, q0, QBLOCK, 0)
        g_blk = lax.dynamic_slice_in_dim(g_all, q0, QBLOCK, 0)
        k_span = lax.dynamic_slice_in_dim(k_ext, q0, span, 0)
        v_span = lax.dynamic_slice_in_dim(v_ext, q0, span, 0)
        qpos = q0 + jnp.arange(QBLOCK, dtype=jnp.int32)
        kpos = q0 - WINDOW + jnp.arange(span, dtype=jnp.int32)
        first = lax.dynamic_slice_in_dim(starts, q0, QBLOCK, 0)
        visible = (kpos[None, :] >= first[:, None]) & (kpos[None, :] <= qpos[:, None]) & (qpos[:, None] - kpos[None, :] < WINDOW)
        bq, bk, bv = block_grads(q_blk, g_blk, k_span, v_span, visible)
        grad_q = lax.dynamic_update_slice_in_dim(grad_q, bq, q0, 0)
        grad_k = lax.dynamic_update_slice_in_dim(grad_k, lax.dynamic_slice_in_dim(grad_k, q0, span, 0) + bk, q0, 0)
        grad_v = lax.dynamic_update_slice_in_dim(grad_v, lax.dynamic_slice_in_dim(grad_v, q0, span, 0) + bv, q0, 0)
        return grad_q, grad_k, grad_v

    init = (jnp.zeros((SEQ_LEN, HEADS, HEAD_DIM), jnp.bfloat16),
            jnp.zeros((WINDOW + SEQ_LEN, HEADS, HEAD_DIM), jnp.float32),
            jnp.zeros((WINDOW + SEQ_LEN, HEADS, HEAD_DIM), jnp.float32))
    grad_q, grad_k, grad_v = lax.fori_loop(0, SEQ_LEN // QBLOCK, step, init)
    head_k = grad_k[WINDOW:].astype(jnp.bfloat16)
    head_v = grad_v[WINDOW:].astype(jnp.bfloat16)
    out_k = head_k.reshape(SEQ_LEN, KV_HEADS, 2, HEAD_DIM).astype(jnp.float32).sum(axis=2).astype(jnp.bfloat16)
    out_v = head_v.reshape(SEQ_LEN, KV_HEADS, 2, HEAD_DIM).astype(jnp.float32).sum(axis=2).astype(jnp.bfloat16)
    return (grad_q.reshape(SEQ_LEN, HEADS * HEAD_DIM),
            out_k.reshape(SEQ_LEN, KV_HEADS * HEAD_DIM),
            out_v.reshape(SEQ_LEN, KV_HEADS * HEAD_DIM))


def reference(query, key, value, grad_out, tile_start):
    grads_q, grads_k, grads_v = [], [], []
    for seq in range(query.shape[0]):
        one_q, one_k, one_v = one_sequence(query[seq], key[seq], value[seq], grad_out[seq], tile_start[seq])
        grads_q.append(one_q)
        grads_k.append(one_k)
        grads_v.append(one_v)
    return (jnp.stack(grads_q), jnp.stack(grads_k), jnp.stack(grads_v))
```

```python
import functools
import math

import jax
import jax.numpy as jnp
from jax import lax
from jax.experimental import pallas as pl
from jax.experimental.pallas import tpu as pltpu
from jax.sharding import PartitionSpec as P

MESH = pl.DeviceIdType.MESH
F32 = jnp.float32
BF16 = jnp.bfloat16

HEAD = 128
TILE = 128
WINDOW = 1024
SEQS = 2
PEERS = 16
BLOCKS = 8
OWN = 1024
ROWS = OWN // PEERS
TILES = OWN // TILE
SPAN = WINDOW + TILE
EXT = WINDOW + OWN
REACH = WINDOW // TILE + 1
NEG = -1e30

score_scale = 168.0 ** (-0.5)
exp2_scale = score_scale * math.log2(math.e)

NT = (((1,), (1,)), ((), ()))
NN = (((1,), (0,)), ((), ()))

K, V, Q, G = range(4)


def dot(a, b, dims):
    return lax.dot_general(a, b, dims, preferred_element_type=F32)


def rows_of(start, size):
    return pl.ds(pl.multiple_of(start, size), size)


def query_tile(i, s, block, starts, qb, gb, kx, vx, kt, sb, db, pb, tb, dka, dva, dqo):
    here = rows_of(i * TILE, TILE)
    span = pl.ds(pl.multiple_of(i * TILE, TILE), SPAN)
    q = qb[s, here, :]
    g = gb[s, here, :]
    q2 = jnp.concatenate([q[:, :HEAD], q[:, HEAD:]], axis=0)
    g2 = jnp.concatenate([g[:, :HEAD], g[:, HEAD:]], axis=0)
    sb[...] = dot(kx[s, span, :], q2, NT)
    db[...] = dot(vx[s, span, :], g2, NT)
    tile = block * TILES + i
    first = starts[s, tile]
    row = lax.broadcasted_iota(jnp.int32, (TILE, 2 * TILE), 0)
    col = lax.broadcasted_iota(jnp.int32, (TILE, 2 * TILE), 1)
    lower = row <= jnp.where(col < TILE, col, col - TILE)
    sb[:TILE] = jnp.where(lower, NEG, sb[:TILE])
    sb[WINDOW:] = jnp.where(lower, sb[WINDOW:], NEG)
    bias = []
    top = None
    for n in range(REACH):
        part = slice(n * TILE, (n + 1) * TILE)
        bias.append(jnp.where(tile - (REACH - 1) + n >= first, 0.0, NEG).astype(F32))
        high = jnp.max(sb[part].reshape(TILE // 8, 8, 2 * TILE), axis=0) + bias[n]
        top = high if top is None else jnp.maximum(top, high)
    top = jnp.max(top, axis=0, keepdims=True) * exp2_scale
    total = jnp.zeros((8, 2 * TILE), F32)
    delta = jnp.zeros((8, 2 * TILE), F32)
    for n in range(REACH):
        part = slice(n * TILE, (n + 1) * TILE)
        weights = jnp.exp2(sb[part] * exp2_scale - (top - bias[n]))
        total = total + jnp.sum(weights.reshape(TILE // 8, 8, 2 * TILE), axis=0)
        delta = delta + jnp.sum((weights * db[part]).reshape(TILE // 8, 8, 2 * TILE), axis=0)
        sb[part] = weights
    inverse = 1.0 / jnp.sum(total, axis=0, keepdims=True)
    delta = jnp.sum(delta, axis=0, keepdims=True) * inverse
    for n in range(REACH):
        part = slice(n * TILE, (n + 1) * TILE)
        probs = sb[part] * inverse
        pb[part] = probs.astype(BF16)
        tb[part] = (probs * (db[part] - delta)).astype(BF16)
    dva[span, :] += dot(pb[...], g2, NN)
    dka[span, :] += dot(tb[...], q2, NN)
    dq = (dot(kt[:, span], tb[...], NN) * score_scale).T
    dqo[s, here, :HEAD] = dq[:TILE].astype(BF16)
    dqo[s, here, HEAD:] = dq[TILE:].astype(BF16)


def kernel(
    starts, q_ref, k_ref, v_ref, g_ref, dq_ref, dk_ref, dv_ref,
    qb, gb, kx, vx, kt, sb, db, pb, tb, dka, dva, hs, hr, dqo, dko, dvo,
    in_recv, in_send, halo_recv, halo_send, back_recv, back_send, out_recv, out_send,
):
    ctx = lax.axis_index("ctx")
    place = lax.axis_index("fsdp")
    me = lax.rem(place, PEERS)
    half = place // PEERS
    block = ctx * 2 + half
    following = (ctx + half, (1 - half) * PEERS + me)
    previous = (ctx - (1 - half), (1 - half) * PEERS + me)
    has_next = block < BLOCKS - 1
    has_prev = block > 0

    def peer(j):
        x = lax.rem(me // 4 + j // 4, 4)
        y = lax.rem(lax.rem(me, 4) + lax.rem(j, 4), 4)
        return x * 4 + y

    def device(p):
        return (ctx, half * PEERS + p)

    barrier = pltpu.get_barrier_semaphore()

    def greet(j, carry):
        pl.semaphore_signal(barrier, inc=1, device_id=device(peer(j)), device_id_type=MESH)
        return carry

    lax.fori_loop(1, PEERS, greet, 0)

    @pl.when(has_next)
    def _():
        pl.semaphore_signal(barrier, inc=1, device_id=following, device_id_type=MESH)

    @pl.when(has_prev)
    def _():
        pl.semaphore_signal(barrier, inc=1, device_id=previous, device_id_type=MESH)

    more = jnp.where(has_next, 1, 0) + jnp.where(has_prev, 1, 0)
    pl.semaphore_wait(barrier, PEERS - 1 + more)

    incoming = {
        K: (k_ref, lambda s: kx.at[s, pl.ds(WINDOW, OWN), :], HEAD),
        V: (v_ref, lambda s: vx.at[s, pl.ds(WINDOW, OWN), :], HEAD),
        Q: (q_ref, lambda s: qb.at[s], 2 * HEAD),
        G: (g_ref, lambda s: gb.at[s], 2 * HEAD),
    }

    def scatter(s, kind):
        ref, buf, width = incoming[kind]
        landing = buf(s).at[rows_of(me * ROWS, ROWS), :]

        def columns(p):
            return ref.at[s, :, rows_of(p * width, width)]

        pltpu.make_async_copy(columns(me), landing, in_recv.at[s, kind]).start()

        def send(j, carry):
            p = peer(j)
            pltpu.make_async_remote_copy(
                columns(p), landing, in_send.at[s, kind], in_recv.at[s, kind],
                device_id=device(p), device_id_type=MESH,
            ).start()
            return carry

        lax.fori_loop(1, PEERS, send, 0)

    for s, kind in ((0, K), (0, V), (1, K), (1, V), (0, Q), (0, G), (1, Q), (1, G)):
        scatter(s, kind)

    @pl.when(jnp.logical_not(has_prev))
    def _():
        kx[:, :WINDOW, :] = jnp.zeros((SEQS, WINDOW, HEAD), BF16)
        vx[:, :WINDOW, :] = jnp.zeros((SEQS, WINDOW, HEAD), BF16)

    @pl.when(jnp.logical_not(has_next))
    def _():
        hr[...] = jnp.zeros_like(hr)

    def arrived(ref, sem):
        pltpu.make_async_copy(ref, ref, sem).wait()

    def forward(s):
        for kind, buf in ((K, kx), (V, vx)):
            own = buf.at[s, pl.ds(WINDOW, OWN), :]
            arrived(own, in_recv.at[s, kind])

            @pl.when(has_next)
            def _():
                pltpu.make_async_remote_copy(
                    own, buf.at[s, pl.ds(0, WINDOW), :], halo_send.at[s, kind], halo_recv.at[s, kind],
                    device_id=following, device_id_type=MESH,
                ).start()

    def compute(s):
        arrived(qb.at[s], in_recv.at[s, Q])
        arrived(gb.at[s], in_recv.at[s, G])
        dka[...] = jnp.zeros_like(dka)
        dva[...] = jnp.zeros_like(dva)

        @pl.when(has_prev)
        def _():
            for kind, buf in ((K, kx), (V, vx)):
                arrived(buf.at[s, pl.ds(0, WINDOW), :], halo_recv.at[s, kind])

        def turn(t, carry):
            part = rows_of(t * TILE, TILE)
            kt[:, part] = kx[s, part, :].T
            return carry

        lax.fori_loop(0, EXT // TILE, turn, 0)

        def step(i, carry):
            query_tile(i, s, block, starts, qb, gb, kx, vx, kt, sb, db, pb, tb, dka, dva, dqo)
            part = rows_of(i * TILE, TILE)
            hs[s, 0, part, :] = (dka[part, :] * score_scale).astype(BF16)
            hs[s, 1, part, :] = dva[part, :].astype(BF16)

            @pl.when(has_prev)
            def _():
                for n in range(2):
                    pltpu.make_async_remote_copy(
                        hs.at[s, n, part, :], hr.at[s, n, part, :], back_send.at[s, n], back_recv.at[s, n],
                        device_id=previous, device_id_type=MESH,
                    ).start()

            return carry

        lax.fori_loop(0, TILES, step, 0)

    def outgoing(s, kind, buf, ref, width):
        columns = ref.at[s, :, rows_of(me * width, width)]
        pltpu.make_async_copy(buf.at[s, rows_of(me * ROWS, ROWS), :], columns, out_recv.at[s, kind]).start()

        def send(j, carry):
            p = peer(j)
            pltpu.make_async_remote_copy(
                buf.at[s, rows_of(p * ROWS, ROWS), :], columns, out_send.at[s, kind], out_recv.at[s, kind],
                device_id=device(p), device_id_type=MESH,
            ).start()
            return carry

        lax.fori_loop(1, PEERS, send, 0)

    forward(0)
    forward(1)
    for s in range(SEQS):
        compute(s)
        outgoing(s, 0, dqo, dq_ref, 2 * HEAD)

        @pl.when(has_next)
        def _():
            for n in range(2):
                arrived(hr.at[s, n], back_recv.at[s, n])

        dko[s] = (dka[WINDOW:, :] * score_scale + hr[s, 0].astype(F32)).astype(BF16)
        dvo[s] = (dva[WINDOW:, :] + hr[s, 1].astype(F32)).astype(BF16)
        outgoing(s, 1, dko, dk_ref, HEAD)
        outgoing(s, 2, dvo, dv_ref, HEAD)

    others = OWN - ROWS
    for s in range(SEQS):
        for kind, ref in ((0, dq_ref), (1, dk_ref), (2, dv_ref)):
            arrived(ref.at[s], out_recv.at[s, kind])
        for kind, buf in ((0, dqo), (1, dko), (2, dvo)):
            arrived(buf.at[s, pl.ds(0, others), :], out_send.at[s, kind])
        for kind, (_, buf, _) in incoming.items():
            arrived(buf(s).at[pl.ds(0, others), :], in_send.at[s, kind])

        @pl.when(has_next)
        def _():
            for kind, buf in ((K, kx), (V, vx)):
                arrived(buf.at[s, pl.ds(0, WINDOW), :], halo_send.at[s, kind])

        @pl.when(has_prev)
        def _():
            for n in range(2):
                arrived(hs.at[s, n], back_send.at[s, n])


def body(query, key, value, grad_out, tile_start):
    dma = pltpu.SemaphoreType.DMA
    hbm = pl.BlockSpec(memory_space=pl.ANY)
    return pl.pallas_call(
        kernel,
        out_shape=(
            jax.ShapeDtypeStruct(query.shape, BF16),
            jax.ShapeDtypeStruct(key.shape, BF16),
            jax.ShapeDtypeStruct(value.shape, BF16),
        ),
        in_specs=[pl.BlockSpec(memory_space=pltpu.SMEM)] + [hbm] * 4,
        out_specs=[hbm] * 3,
        scratch_shapes=[
            pltpu.VMEM((SEQS, OWN, 2 * HEAD), BF16),
            pltpu.VMEM((SEQS, OWN, 2 * HEAD), BF16),
            pltpu.VMEM((SEQS, EXT, HEAD), BF16),
            pltpu.VMEM((SEQS, EXT, HEAD), BF16),
            pltpu.VMEM((HEAD, EXT), BF16),
            pltpu.VMEM((SPAN, 2 * TILE), F32),
            pltpu.VMEM((SPAN, 2 * TILE), F32),
            pltpu.VMEM((SPAN, 2 * TILE), BF16),
            pltpu.VMEM((SPAN, 2 * TILE), BF16),
            pltpu.VMEM((EXT, HEAD), F32),
            pltpu.VMEM((EXT, HEAD), F32),
            pltpu.VMEM((SEQS, 2, WINDOW, HEAD), BF16),
            pltpu.VMEM((SEQS, 2, WINDOW, HEAD), BF16),
            pltpu.VMEM((SEQS, OWN, 2 * HEAD), BF16),
            pltpu.VMEM((SEQS, OWN, HEAD), BF16),
            pltpu.VMEM((SEQS, OWN, HEAD), BF16),
            dma((SEQS, 4)), dma((SEQS, 4)),
            dma((SEQS, 2)), dma((SEQS, 2)),
            dma((SEQS, 2)), dma((SEQS, 2)),
            dma((SEQS, 3)), dma((SEQS, 3)),
        ],
        compiler_params=pltpu.CompilerParams(
            collective_id=0, has_side_effects=True, vmem_limit_bytes=48 * 2**20
        ),
        name="attention_grads",
    )(tile_start, query, key, value, grad_out)


def solution(mesh):
    spread = P(None, ("ctx", "fsdp"), None)
    return jax.shard_map(
        body, mesh=mesh, in_specs=(spread,) * 4 + (P(),), out_specs=(spread,) * 3, check_vma=False
    )
```

```python
import functools
import math

import jax
import jax.numpy as jnp
from jax import lax
from jax.experimental import pallas as pl
from jax.experimental.pallas import tpu as pltpu
from jax.sharding import PartitionSpec as P

MESH = pl.DeviceIdType.MESH
F32 = jnp.float32
BF16 = jnp.bfloat16

HEAD = 128
TILE = 128
WINDOW = 1024
SEQS = 2
PEERS = 16
BLOCKS = 8
OWN = 1024
ROWS = OWN // PEERS
TILES = OWN // TILE
QUERIES = 256
STEPS = OWN // QUERIES
LATE = 1
EDGE = QUERIES // TILE
SPAN = WINDOW + QUERIES
EXT = WINDOW + OWN
NEG = -1e30

score_scale = 168.0 ** (-0.5)
exp2_scale = score_scale * math.log2(math.e)

NT = (((1,), (1,)), ((), ()))
NN = (((1,), (0,)), ((), ()))

K, V, Q, G = range(4)
ARRIVALS = (
    [(s, kind) for s in range(SEQS) for kind in (K, V)]
    + [(s, kind + 2 * h) for s in range(SEQS) for h in range(2) for kind in (Q, G)]
)


def dot(a, b, dims):
    return lax.dot_general(a, b, dims, preferred_element_type=F32)


def rows_of(start, size):
    return pl.ds(pl.multiple_of(start, size), size)


def fold(x):
    return x.reshape(x.shape[0] // 8, 8, QUERIES)


def lower_of(n):
    row = lax.broadcasted_iota(jnp.int32, (TILE, QUERIES), 0) + n * TILE
    return row <= lax.broadcasted_iota(jnp.int32, (TILE, QUERIES), 1)


def query_step(i, s, h, block, starts, qb, gb, kx, vx, kt, sb, db, pb, tb, dka, dva, dqo):
    here = rows_of(i * QUERIES, QUERIES)
    span = pl.ds(pl.multiple_of(i * QUERIES, QUERIES), SPAN)
    q = qb[s, h, here, :]
    g = gb[s, h, here, :]
    sb[...] = dot(kx[s, span, :], q, NT)
    db[...] = dot(vx[s, span, :], g, NT)
    lane = lax.broadcasted_iota(jnp.int32, (1, QUERIES), 1)
    tile = block * TILES + 2 * i
    first = [starts[s, tile], starts[s, tile + 1]]
    bias = []
    for n in range(SPAN // TILE):
        key_tile = tile - WINDOW // TILE + n
        seen = [jnp.where(key_tile >= f, 0.0, NEG).astype(F32) for f in first]
        bias.append(jnp.where(lane < TILE, seen[0], seen[1]))
    top = None
    for n in range(WINDOW // TILE):
        part = slice(n * TILE, (n + 1) * TILE)
        if n < EDGE:
            lower = lower_of(n)
            near = slice(WINDOW + n * TILE, WINDOW + (n + 1) * TILE)
            merged = jnp.where(lower, sb[near] + bias[WINDOW // TILE + n], sb[part] + bias[n])
            sb[part] = merged
            db[part] = jnp.where(lower, db[near], db[part])
            high = jnp.max(fold(merged), axis=0)
        else:
            high = jnp.max(fold(sb[part]), axis=0) + bias[n]
        top = high if top is None else jnp.maximum(top, high)
    top = jnp.max(top, axis=0, keepdims=True) * exp2_scale
    total = jnp.zeros((8, QUERIES), F32)
    delta = jnp.zeros((8, QUERIES), F32)
    for n in range(WINDOW // TILE):
        part = slice(n * TILE, (n + 1) * TILE)
        weights = jnp.exp2(sb[part] * exp2_scale - (top if n < EDGE else top - bias[n]))
        total = total + jnp.sum(fold(weights), axis=0)
        delta = delta + jnp.sum(fold(weights * db[part]), axis=0)
        sb[part] = weights
    inverse = 1.0 / jnp.sum(total, axis=0, keepdims=True)
    delta = jnp.sum(delta, axis=0, keepdims=True) * inverse
    for n in range(WINDOW // TILE):
        part = slice(n * TILE, (n + 1) * TILE)
        probs = sb[part] * inverse
        grads = probs * (db[part] - delta)
        if n < EDGE:
            lower = lower_of(n)
            near = slice(WINDOW + n * TILE, WINDOW + (n + 1) * TILE)
            pb[near] = jnp.where(lower, probs, 0.0).astype(BF16)
            tb[near] = jnp.where(lower, grads, 0.0).astype(BF16)
            pb[part] = jnp.where(lower, 0.0, probs).astype(BF16)
            tb[part] = jnp.where(lower, 0.0, grads).astype(BF16)
        else:
            pb[part] = probs.astype(BF16)
            tb[part] = grads.astype(BF16)
    dva[s, span, :] += dot(pb[...], g, NN)
    dka[s, span, :] += dot(tb[...], q, NN)
    dqo[s, h, here, :] = (dot(kt[:, span], tb[...], NN) * score_scale).T.astype(BF16)


def kernel(
    starts, q_ref, k_ref, v_ref, g_ref, dq_ref, dk_ref, dv_ref,
    qb, gb, kx, vx, kt, sb, db, pb, tb, dka, dva, hs, hr, dqo, dko, dvo,
    in_recv, in_send, halo_recv, halo_send, back_recv, back_send, out_recv, out_send,
):
    ctx = lax.axis_index("ctx")
    place = lax.axis_index("fsdp")
    me = lax.rem(place, PEERS)
    half = place // PEERS
    block = ctx * 2 + half
    following = (ctx + half, (1 - half) * PEERS + me)
    previous = (ctx - (1 - half), (1 - half) * PEERS + me)
    has_next = block < BLOCKS - 1
    has_prev = block > 0

    def peer(j):
        x = lax.rem(me // 4 + j // 4, 4)
        y = lax.rem(lax.rem(me, 4) + lax.rem(j, 4), 4)
        return x * 4 + y

    def device(p):
        return (ctx, half * PEERS + p)

    barrier = pltpu.get_barrier_semaphore()

    def greet(j, carry):
        pl.semaphore_signal(barrier, inc=1, device_id=device(peer(j)), device_id_type=MESH)
        return carry

    lax.fori_loop(1, PEERS, greet, 0)

    @pl.when(has_next)
    def _():
        pl.semaphore_signal(barrier, inc=1, device_id=following, device_id_type=MESH)

    @pl.when(has_prev)
    def _():
        pl.semaphore_signal(barrier, inc=1, device_id=previous, device_id_type=MESH)

    more = jnp.where(has_next, 1, 0) + jnp.where(has_prev, 1, 0)
    pl.semaphore_wait(barrier, PEERS - 1 + more)

    def keys_of(ref, buf):
        def source(s, p):
            return ref.at[s, :, rows_of(p * HEAD, HEAD)]

        return source, lambda s: buf.at[s, pl.ds(WINDOW, OWN), :]

    def heads_of(ref, buf, h):
        def source(s, p):
            return ref.at[s, :, rows_of((2 * p + h) * HEAD, HEAD)]

        return source, lambda s: buf.at[s, h]

    incoming = {
        K: keys_of(k_ref, kx),
        V: keys_of(v_ref, vx),
        Q: heads_of(q_ref, qb, 0),
        G: heads_of(g_ref, gb, 0),
        Q + 2: heads_of(q_ref, qb, 1),
        G + 2: heads_of(g_ref, gb, 1),
    }

    def scatter(s, kind):
        source, buf = incoming[kind]
        landing = buf(s).at[rows_of(me * ROWS, ROWS), :]
        pltpu.make_async_copy(source(s, me), landing, in_recv.at[s, kind]).start()

        def send(j, carry):
            p = peer(j)
            pltpu.make_async_remote_copy(
                source(s, p), landing, in_send.at[s, kind], in_recv.at[s, kind],
                device_id=device(p), device_id_type=MESH,
            ).start()
            return carry

        lax.fori_loop(1, PEERS, send, 0)

    for s, kind in ARRIVALS:
        scatter(s, kind)

    @pl.when(jnp.logical_not(has_prev))
    def _():
        kx[:, :WINDOW, :] = jnp.zeros((SEQS, WINDOW, HEAD), BF16)
        vx[:, :WINDOW, :] = jnp.zeros((SEQS, WINDOW, HEAD), BF16)

    @pl.when(jnp.logical_not(has_next))
    def _():
        hr[...] = jnp.zeros_like(hr)

    def arrived(ref, sem):
        pltpu.make_async_copy(ref, ref, sem).wait()

    def forward(s):
        for kind, buf in ((K, kx), (V, vx)):
            own = buf.at[s, pl.ds(WINDOW, OWN), :]
            arrived(own, in_recv.at[s, kind])

            @pl.when(has_next)
            def _():
                pltpu.make_async_remote_copy(
                    own, buf.at[s, pl.ds(0, WINDOW), :], halo_send.at[s, kind], halo_recv.at[s, kind],
                    device_id=following, device_id_type=MESH,
                ).start()

    def outgoing(s, kind, buf, columns):
        pltpu.make_async_copy(buf.at[rows_of(me * ROWS, ROWS), :], columns, out_recv.at[s, kind]).start()

        def send(j, carry):
            p = peer(j)
            pltpu.make_async_remote_copy(
                buf.at[rows_of(p * ROWS, ROWS), :], columns, out_send.at[s, kind], out_recv.at[s, kind],
                device_id=device(p), device_id_type=MESH,
            ).start()
            return carry

        lax.fori_loop(1, PEERS, send, 0)

    mine = rows_of(me * HEAD, HEAD)

    def finish(s):
        @pl.when(has_next)
        def _():
            for n in range(2):
                arrived(hr.at[s, n], back_recv.at[s, n])

        dko[s] = (dka[s, WINDOW:, :] * score_scale + hr[s, 0].astype(F32)).astype(BF16)
        outgoing(s, 2, dko.at[s], dk_ref.at[s, :, mine])
        dvo[s] = (dva[s, WINDOW:, :] + hr[s, 1].astype(F32)).astype(BF16)
        outgoing(s, 3, dvo.at[s], dv_ref.at[s, :, mine])

    def compute(s):
        dka[s] = jnp.zeros((EXT, HEAD), F32)
        dva[s] = jnp.zeros((EXT, HEAD), F32)

        @pl.when(has_prev)
        def _():
            for kind, buf in ((K, kx), (V, vx)):
                arrived(buf.at[s, pl.ds(0, WINDOW), :], halo_recv.at[s, kind])

        def turn(t, carry):
            part = rows_of(t * TILE, TILE)
            kt[:, part] = kx[s, part, :].T
            return carry

        lax.fori_loop(0, EXT // TILE, turn, 0)

        def head(h, carry):
            arrived(qb.at[s, h], in_recv.at[s, Q + 2 * h])
            arrived(gb.at[s, h], in_recv.at[s, G + 2 * h])

            def step(i, inner):
                query_step(i, s, h, block, starts, qb, gb, kx, vx, kt, sb, db, pb, tb, dka, dva, dqo)

                @pl.when(h == 1)
                def _():
                    part = rows_of(i * QUERIES, QUERIES)
                    hs[s, 0, part, :] = (dka[s, part, :] * score_scale).astype(BF16)
                    hs[s, 1, part, :] = dva[s, part, :].astype(BF16)

                    @pl.when(has_prev)
                    def _():
                        for n in range(2):
                            pltpu.make_async_remote_copy(
                                hs.at[s, n, part, :], hr.at[s, n, part, :], back_send.at[s, n], back_recv.at[s, n],
                                device_id=previous, device_id_type=MESH,
                            ).start()

                if s > 0:
                    @pl.when(jnp.logical_and(h == 1, i == LATE))
                    def _():
                        finish(s - 1)

                return inner

            lax.fori_loop(0, STEPS, step, 0)
            outgoing(s, h, dqo.at[s, h], dq_ref.at[s, :, rows_of((2 * me + h) * HEAD, HEAD)])
            return carry

        lax.fori_loop(0, 2, head, 0)

    forward(0)
    forward(1)
    compute(0)
    compute(1)
    finish(1)

    others = pl.ds(0, OWN - ROWS)
    for s in range(SEQS):
        for h in range(2):
            arrived(dq_ref.at[s, :, pl.ds(0, PEERS * HEAD)], out_recv.at[s, h])
        arrived(dk_ref.at[s], out_recv.at[s, 2])
        arrived(dv_ref.at[s], out_recv.at[s, 3])
        for kind, buf in enumerate((dqo.at[s, 0], dqo.at[s, 1], dko.at[s], dvo.at[s])):
            arrived(buf.at[others, :], out_send.at[s, kind])
        for kind, (_, buf) in incoming.items():
            arrived(buf(s).at[others, :], in_send.at[s, kind])

        @pl.when(has_next)
        def _():
            for kind, buf in ((K, kx), (V, vx)):
                arrived(buf.at[s, pl.ds(0, WINDOW), :], halo_send.at[s, kind])

        @pl.when(has_prev)
        def _():
            for n in range(2):
                arrived(hs.at[s, n], back_send.at[s, n])


def body(query, key, value, grad_out, tile_start):
    dma = pltpu.SemaphoreType.DMA
    hbm = pl.BlockSpec(memory_space=pl.ANY)
    return pl.pallas_call(
        kernel,
        out_shape=(
            jax.ShapeDtypeStruct(query.shape, BF16),
            jax.ShapeDtypeStruct(key.shape, BF16),
            jax.ShapeDtypeStruct(value.shape, BF16),
        ),
        in_specs=[pl.BlockSpec(memory_space=pltpu.SMEM)] + [hbm] * 4,
        out_specs=[hbm] * 3,
        scratch_shapes=[
            pltpu.VMEM((SEQS, 2, OWN, HEAD), BF16),
            pltpu.VMEM((SEQS, 2, OWN, HEAD), BF16),
            pltpu.VMEM((SEQS, EXT, HEAD), BF16),
            pltpu.VMEM((SEQS, EXT, HEAD), BF16),
            pltpu.VMEM((HEAD, EXT), BF16),
            pltpu.VMEM((SPAN, QUERIES), F32),
            pltpu.VMEM((SPAN, QUERIES), F32),
            pltpu.VMEM((SPAN, QUERIES), BF16),
            pltpu.VMEM((SPAN, QUERIES), BF16),
            pltpu.VMEM((SEQS, EXT, HEAD), F32),
            pltpu.VMEM((SEQS, EXT, HEAD), F32),
            pltpu.VMEM((SEQS, 2, WINDOW, HEAD), BF16),
            pltpu.VMEM((SEQS, 2, WINDOW, HEAD), BF16),
            pltpu.VMEM((SEQS, 2, OWN, HEAD), BF16),
            pltpu.VMEM((SEQS, OWN, HEAD), BF16),
            pltpu.VMEM((SEQS, OWN, HEAD), BF16),
            dma((SEQS, 6)), dma((SEQS, 6)),
            dma((SEQS, 2)), dma((SEQS, 2)),
            dma((SEQS, 2)), dma((SEQS, 2)),
            dma((SEQS, 4)), dma((SEQS, 4)),
        ],
        compiler_params=pltpu.CompilerParams(
            collective_id=0, has_side_effects=True, vmem_limit_bytes=67043328
        ),
        name="attention_grads",
    )(tile_start, query, key, value, grad_out)


def solution(mesh):
    spread = P(None, ("ctx", "fsdp"), None)
    return jax.shard_map(
        body, mesh=mesh, in_specs=(spread,) * 4 + (P(),), out_specs=(spread,) * 3, check_vma=False
    )
```

```python
import functools
import math

import jax
import jax.numpy as jnp
from jax import lax
from jax.experimental import pallas as pl
from jax.experimental.pallas import tpu as pltpu
from jax.sharding import PartitionSpec as P

MESH = pl.DeviceIdType.MESH
F32 = jnp.float32
BF16 = jnp.bfloat16

HEAD = 128
TILE = 128
WINDOW = 1024
SEQS = 2
PEERS = 16
BLOCKS = 8
OWN = 1024
ROWS = OWN // PEERS
TILES = OWN // TILE
QUERIES = 256
STEPS = OWN // QUERIES
LATE = 1
EDGE = QUERIES // TILE
SPAN = WINDOW + QUERIES
EXT = WINDOW + OWN
NEG = -1e30

score_scale = 168.0 ** (-0.5)
exp2_scale = score_scale * math.log2(math.e)

NT = (((1,), (1,)), ((), ()))
NN = (((1,), (0,)), ((), ()))

K, V, Q, G = range(4)
ARRIVALS = (
    [(s, kind) for s in range(SEQS) for kind in (K, V)]
    + [(s, kind + 2 * h) for s in range(SEQS) for h in range(2) for kind in (Q, G)]
)


def dot(a, b, dims):
    return lax.dot_general(a, b, dims, preferred_element_type=F32)


def rows_of(start, size):
    return pl.ds(pl.multiple_of(start, size), size)


def fold(x):
    return x.reshape(x.shape[0] // 8, 8, QUERIES)


def lower_of(n):
    row = lax.broadcasted_iota(jnp.int32, (TILE, QUERIES), 0) + n * TILE
    return row <= lax.broadcasted_iota(jnp.int32, (TILE, QUERIES), 1)


def query_step(i, s, h, block, starts, qb, gb, kx, vx, kt, sb, db, pb, tb, dka, dva, dqo):
    here = rows_of(i * QUERIES, QUERIES)
    span = pl.ds(pl.multiple_of(i * QUERIES, QUERIES), SPAN)
    q = qb[s, h, here, :]
    g = gb[s, h, here, :]
    sb[...] = dot(kx[s, span, :], q, NT)
    db[...] = dot(vx[s, span, :], g, NT)
    lane = lax.broadcasted_iota(jnp.int32, (1, QUERIES), 1)
    tile = block * TILES + 2 * i
    first = [starts[s, tile], starts[s, tile + 1]]
    bias = []
    for n in range(SPAN // TILE):
        key_tile = tile - WINDOW // TILE + n
        seen = [jnp.where(key_tile >= f, 0.0, NEG).astype(F32) for f in first]
        bias.append(jnp.where(lane < TILE, seen[0], seen[1]))
    top = None
    for n in range(WINDOW // TILE):
        part = slice(n * TILE, (n + 1) * TILE)
        if n < EDGE:
            lower = lower_of(n)
            near = slice(WINDOW + n * TILE, WINDOW + (n + 1) * TILE)
            merged = jnp.where(lower, sb[near] + bias[WINDOW // TILE + n], sb[part] + bias[n])
            sb[part] = merged
            db[part] = jnp.where(lower, db[near], db[part])
            high = jnp.max(fold(merged), axis=0)
        else:
            high = jnp.max(fold(sb[part]), axis=0) + bias[n]
        top = high if top is None else jnp.maximum(top, high)
    top = jnp.max(top, axis=0, keepdims=True) * exp2_scale
    total = jnp.zeros((8, QUERIES), F32)
    delta = jnp.zeros((8, QUERIES), F32)
    for n in range(WINDOW // TILE):
        part = slice(n * TILE, (n + 1) * TILE)
        weights = jnp.exp2(sb[part] * exp2_scale - (top if n < EDGE else top - bias[n]))
        total = total + jnp.sum(fold(weights), axis=0)
        delta = delta + jnp.sum(fold(weights * db[part]), axis=0)
        sb[part] = weights
    inverse = 1.0 / jnp.sum(total, axis=0, keepdims=True)
    delta = jnp.sum(delta, axis=0, keepdims=True) * inverse
    for n in range(WINDOW // TILE):
        part = slice(n * TILE, (n + 1) * TILE)
        probs = sb[part] * inverse
        grads = probs * (db[part] - delta)
        if n < EDGE:
            lower = lower_of(n)
            near = slice(WINDOW + n * TILE, WINDOW + (n + 1) * TILE)
            pb[near] = jnp.where(lower, probs, 0.0).astype(BF16)
            tb[near] = jnp.where(lower, grads, 0.0).astype(BF16)
            pb[part] = jnp.where(lower, 0.0, probs).astype(BF16)
            tb[part] = jnp.where(lower, 0.0, grads).astype(BF16)
        else:
            pb[part] = probs.astype(BF16)
            tb[part] = grads.astype(BF16)
    dva[s, span, :] += dot(pb[...], g, NN)
    dka[s, span, :] += dot(tb[...], q, NN)
    dqo[s, h, here, :] = (dot(kt[:, span], tb[...], NN) * score_scale).T.astype(BF16)


def kernel(
    starts, q_ref, k_ref, v_ref, g_ref, dq_ref, dk_ref, dv_ref,
    qb, gb, kx, vx, kt, sb, db, pb, tb, dka, dva, hs, hr, dqo, dko, dvo,
    in_recv, in_send, halo_recv, halo_send, back_recv, back_send, out_recv, out_send,
):
    ctx = lax.axis_index("ctx")
    place = lax.axis_index("fsdp")
    me = lax.rem(place, PEERS)
    half = place // PEERS
    block = ctx * 2 + half
    following = (ctx + half, (1 - half) * PEERS + me)
    previous = (ctx - (1 - half), (1 - half) * PEERS + me)
    has_next = block < BLOCKS - 1
    has_prev = block > 0

    def peer(j):
        x = lax.rem(me // 4 + j // 4, 4)
        y = lax.rem(lax.rem(me, 4) + lax.rem(j, 4), 4)
        return x * 4 + y

    def device(p):
        return (ctx, half * PEERS + p)

    barrier = pltpu.get_barrier_semaphore()

    def greet(j, carry):
        pl.semaphore_signal(barrier, inc=1, device_id=device(peer(j)), device_id_type=MESH)
        return carry

    lax.fori_loop(1, PEERS, greet, 0)

    @pl.when(has_next)
    def _():
        pl.semaphore_signal(barrier, inc=1, device_id=following, device_id_type=MESH)

    @pl.when(has_prev)
    def _():
        pl.semaphore_signal(barrier, inc=1, device_id=previous, device_id_type=MESH)

    more = jnp.where(has_next, 1, 0) + jnp.where(has_prev, 1, 0)
    pl.semaphore_wait(barrier, PEERS - 1 + more)

    def keys_of(ref, buf):
        def source(s, p):
            return ref.at[s, :, rows_of(p * HEAD, HEAD)]

        return source, lambda s: buf.at[s, pl.ds(WINDOW, OWN), :]

    def heads_of(ref, buf, h):
        def source(s, p):
            return ref.at[s, :, rows_of((2 * p + h) * HEAD, HEAD)]

        return source, lambda s: buf.at[s, h]

    incoming = {
        K: keys_of(k_ref, kx),
        V: keys_of(v_ref, vx),
        Q: heads_of(q_ref, qb, 0),
        G: heads_of(g_ref, gb, 0),
        Q + 2: heads_of(q_ref, qb, 1),
        G + 2: heads_of(g_ref, gb, 1),
    }

    def scatter(s, kind):
        source, buf = incoming[kind]
        landing = buf(s).at[rows_of(me * ROWS, ROWS), :]
        pltpu.make_async_copy(source(s, me), landing, in_recv.at[s, kind]).start()

        def send(j, carry):
            p = peer(j)
            pltpu.make_async_remote_copy(
                source(s, p), landing, in_send.at[s, kind], in_recv.at[s, kind],
                device_id=device(p), device_id_type=MESH,
            ).start()
            return carry

        lax.fori_loop(1, PEERS, send, 0)

    for s, kind in ARRIVALS:
        scatter(s, kind)

    @pl.when(jnp.logical_not(has_prev))
    def _():
        kx[:, :WINDOW, :] = jnp.zeros((SEQS, WINDOW, HEAD), BF16)
        vx[:, :WINDOW, :] = jnp.zeros((SEQS, WINDOW, HEAD), BF16)

    @pl.when(jnp.logical_not(has_next))
    def _():
        hr[...] = jnp.zeros_like(hr)

    def arrived(ref, sem):
        pltpu.make_async_copy(ref, ref, sem).wait()

    def forward(s):
        for kind, buf in ((K, kx), (V, vx)):
            own = buf.at[s, pl.ds(WINDOW, OWN), :]
            arrived(own, in_recv.at[s, kind])

            @pl.when(has_next)
            def _():
                pltpu.make_async_remote_copy(
                    own, buf.at[s, pl.ds(0, WINDOW), :], halo_send.at[s, kind], halo_recv.at[s, kind],
                    device_id=following, device_id_type=MESH,
                ).start()

    def outgoing(s, kind, buf, columns):
        pltpu.make_async_copy(buf.at[rows_of(me * ROWS, ROWS), :], columns, out_recv.at[s, kind]).start()

        def send(j, carry):
            p = peer(j)
            pltpu.make_async_remote_copy(
                buf.at[rows_of(p * ROWS, ROWS), :], columns, out_send.at[s, kind], out_recv.at[s, kind],
                device_id=device(p), device_id_type=MESH,
            ).start()
            return carry

        lax.fori_loop(1, PEERS, send, 0)

    mine = rows_of(me * HEAD, HEAD)

    def finish(s):
        @pl.when(has_next)
        def _():
            for n in range(2):
                arrived(hr.at[s, n], back_recv.at[s, n])

        dko[s] = (dka[s, WINDOW:, :] * score_scale + hr[s, 0].astype(F32)).astype(BF16)
        outgoing(s, 2, dko.at[s], dk_ref.at[s, :, mine])
        dvo[s] = (dva[s, WINDOW:, :] + hr[s, 1].astype(F32)).astype(BF16)
        outgoing(s, 3, dvo.at[s], dv_ref.at[s, :, mine])

    def compute(s):
        dka[s] = jnp.zeros((EXT, HEAD), F32)
        dva[s] = jnp.zeros((EXT, HEAD), F32)

        @pl.when(has_prev)
        def _():
            for kind, buf in ((K, kx), (V, vx)):
                arrived(buf.at[s, pl.ds(0, WINDOW), :], halo_recv.at[s, kind])

        def turn(t, carry):
            part = rows_of(t * TILE, TILE)
            kt[:, part] = kx[s, part, :].T
            return carry

        lax.fori_loop(0, EXT // TILE, turn, 0)

        def head(h, carry):
            arrived(qb.at[s, h], in_recv.at[s, Q + 2 * h])
            arrived(gb.at[s, h], in_recv.at[s, G + 2 * h])

            def step(i, inner):
                query_step(i, s, h, block, starts, qb, gb, kx, vx, kt, sb, db, pb, tb, dka, dva, dqo)

                @pl.when(h == 1)
                def _():
                    part = rows_of(i * QUERIES, QUERIES)
                    hs[s, 0, part, :] = (dka[s, part, :] * score_scale).astype(BF16)
                    hs[s, 1, part, :] = dva[s, part, :].astype(BF16)

                    @pl.when(has_prev)
                    def _():
                        for n in range(2):
                            pltpu.make_async_remote_copy(
                                hs.at[s, n, part, :], hr.at[s, n, part, :], back_send.at[s, n], back_recv.at[s, n],
                                device_id=previous, device_id_type=MESH,
                            ).start()

                if s > 0:
                    @pl.when(jnp.logical_and(h == 1, i == LATE))
                    def _():
                        finish(s - 1)

                return inner

            lax.fori_loop(0, STEPS, step, 0)
            outgoing(s, h, dqo.at[s, h], dq_ref.at[s, :, rows_of((2 * me + h) * HEAD, HEAD)])
            return carry

        lax.fori_loop(0, 2, head, 0)

    forward(0)
    forward(1)
    compute(0)
    compute(1)
    finish(1)

    others = pl.ds(0, OWN - ROWS)
    for s in range(SEQS):
        for h in range(2):
            arrived(dq_ref.at[s, :, pl.ds(0, PEERS * HEAD)], out_recv.at[s, h])
        arrived(dk_ref.at[s], out_recv.at[s, 2])
        arrived(dv_ref.at[s], out_recv.at[s, 3])
        for kind, buf in enumerate((dqo.at[s, 0], dqo.at[s, 1], dko.at[s], dvo.at[s])):
            arrived(buf.at[others, :], out_send.at[s, kind])
        for kind, (_, buf) in incoming.items():
            arrived(buf(s).at[others, :], in_send.at[s, kind])

        @pl.when(has_next)
        def _():
            for kind, buf in ((K, kx), (V, vx)):
                arrived(buf.at[s, pl.ds(0, WINDOW), :], halo_send.at[s, kind])

        @pl.when(has_prev)
        def _():
            for n in range(2):
                arrived(hs.at[s, n], back_send.at[s, n])


def body(query, key, value, grad_out, tile_start):
    dma = pltpu.SemaphoreType.DMA
    hbm = pl.BlockSpec(memory_space=pl.ANY)
    grads = pl.pallas_call(
        kernel,
        out_shape=(
            pltpu.VMEM(query.shape, BF16),
            pltpu.VMEM(key.shape, BF16),
            pltpu.VMEM(value.shape, BF16),
        ),
        in_specs=[pl.BlockSpec(memory_space=pltpu.SMEM)] + [hbm] * 4,
        out_specs=[hbm] * 3,
        scratch_shapes=[
            pltpu.VMEM((SEQS, 2, OWN, HEAD), BF16),
            pltpu.VMEM((SEQS, 2, OWN, HEAD), BF16),
            pltpu.VMEM((SEQS, EXT, HEAD), BF16),
            pltpu.VMEM((SEQS, EXT, HEAD), BF16),
            pltpu.VMEM((HEAD, EXT), BF16),
            pltpu.VMEM((SPAN, QUERIES), F32),
            pltpu.VMEM((SPAN, QUERIES), F32),
            pltpu.VMEM((SPAN, QUERIES), BF16),
            pltpu.VMEM((SPAN, QUERIES), BF16),
            pltpu.VMEM((SEQS, EXT, HEAD), F32),
            pltpu.VMEM((SEQS, EXT, HEAD), F32),
            pltpu.VMEM((SEQS, 2, WINDOW, HEAD), BF16),
            pltpu.VMEM((SEQS, 2, WINDOW, HEAD), BF16),
            pltpu.VMEM((SEQS, 2, OWN, HEAD), BF16),
            pltpu.VMEM((SEQS, OWN, HEAD), BF16),
            pltpu.VMEM((SEQS, OWN, HEAD), BF16),
            dma((SEQS, 6)), dma((SEQS, 6)),
            dma((SEQS, 2)), dma((SEQS, 2)),
            dma((SEQS, 2)), dma((SEQS, 2)),
            dma((SEQS, 4)), dma((SEQS, 4)),
        ],
        compiler_params=pltpu.CompilerParams(
            collective_id=0, has_side_effects=True, vmem_limit_bytes=64400000
        ),
        name="attention_grads",
    )(tile_start, query, key, value, grad_out)
    return placed(grads)


def place(dq_in, dk_in, dv_in, dq_out, dk_out, dv_out, left):
    copies = [
        pltpu.make_async_copy(ref, out, left.at[n])
        for n, (ref, out) in enumerate(((dq_in, dq_out), (dk_in, dk_out), (dv_in, dv_out)))
    ]
    for copy in copies:
        copy.start()
    for copy in copies:
        copy.wait()


def placed(grads):
    dma = pltpu.SemaphoreType.DMA
    hbm = pl.BlockSpec(memory_space=pl.ANY)
    return pl.pallas_call(
        place,
        out_shape=tuple(jax.ShapeDtypeStruct(g.shape, g.dtype) for g in grads),
        in_specs=[hbm] * 3,
        out_specs=[hbm] * 3,
        scratch_shapes=[dma((3,))],
        compiler_params=pltpu.CompilerParams(vmem_limit_bytes=2**20),
        name="place_grads",
    )(*grads)


def solution(mesh):
    spread = P(None, ("ctx", "fsdp"), None)
    return jax.shard_map(
        body, mesh=mesh, in_specs=(spread,) * 4 + (P(),), out_specs=(spread,) * 3, check_vma=False
    )
```

```python
import functools
import math

import jax
import jax.numpy as jnp
from jax import lax
from jax.experimental import pallas as pl
from jax.experimental.pallas import tpu as pltpu
from jax.sharding import PartitionSpec as P

MESH = pl.DeviceIdType.MESH
F32 = jnp.float32
BF16 = jnp.bfloat16

HEAD = 128
TILE = 128
WINDOW = 1024
SEQS = 2
PEERS = 16
BLOCKS = 8
OWN = 1024
ROWS = OWN // PEERS
TILES = OWN // TILE
QUERIES = 256
STEPS = OWN // QUERIES
LATE = 1
EDGE = QUERIES // TILE
SPAN = WINDOW + QUERIES
EXT = WINDOW + OWN
NEG = -1e30

score_scale = 168.0 ** (-0.5)
exp2_scale = score_scale * math.log2(math.e)

NT = (((1,), (1,)), ((), ()))
NN = (((1,), (0,)), ((), ()))

K, V, Q, G = range(4)
ARRIVALS = (
    [(s, kind) for s in range(SEQS) for kind in (K, V)]
    + [(s, kind + 2 * h) for s in range(SEQS) for h in range(2) for kind in (Q, G)]
)


def dot(a, b, dims):
    return lax.dot_general(a, b, dims, preferred_element_type=F32)


def rows_of(start, size):
    return pl.ds(pl.multiple_of(start, size), size)


def fold(x):
    return x.reshape(x.shape[0] // 8, 8, QUERIES)


def lower_of(n):
    row = lax.broadcasted_iota(jnp.int32, (TILE, QUERIES), 0) + n * TILE
    return row <= lax.broadcasted_iota(jnp.int32, (TILE, QUERIES), 1)


def spans(i):
    return pl.ds(i * QUERIES, QUERIES), pl.ds(i * QUERIES, SPAN)


def scores(i, q, g, keys, values, sb, db):
    here, span = spans(i)
    sb[...] = dot(keys[span, :], q[here, :], NT)
    db[...] = dot(values[span, :], g[here, :], NT)


def score_grads(i, starts, block, sb, db, pb, tb):
    lane = lax.broadcasted_iota(jnp.int32, (1, QUERIES), 1)
    tile = block * TILES + EDGE * i
    first = [starts[tile], starts[tile + 1]]
    bias = []
    for n in range(SPAN // TILE):
        key_tile = tile - WINDOW // TILE + n
        seen = [jnp.where(key_tile >= f, 0.0, NEG).astype(F32) for f in first]
        bias.append(jnp.where(lane < TILE, seen[0], seen[1]))
    top = None
    for n in range(WINDOW // TILE):
        part = slice(n * TILE, (n + 1) * TILE)
        if n < EDGE:
            lower = lower_of(n)
            near = slice(WINDOW + n * TILE, WINDOW + (n + 1) * TILE)
            merged = jnp.where(lower, sb[near] + bias[WINDOW // TILE + n], sb[part] + bias[n])
            sb[part] = merged
            db[part] = jnp.where(lower, db[near], db[part])
            high = jnp.max(fold(merged), axis=0)
        else:
            high = jnp.max(fold(sb[part]), axis=0) + bias[n]
        top = high if top is None else jnp.maximum(top, high)
    top = jnp.max(top, axis=0, keepdims=True) * exp2_scale
    total = jnp.zeros((8, QUERIES), F32)
    delta = jnp.zeros((8, QUERIES), F32)
    for n in range(WINDOW // TILE):
        part = slice(n * TILE, (n + 1) * TILE)
        weights = jnp.exp2(sb[part] * exp2_scale - (top if n < EDGE else top - bias[n]))
        total = total + jnp.sum(fold(weights), axis=0)
        delta = delta + jnp.sum(fold(weights * db[part]), axis=0)
        sb[part] = weights
    inverse = 1.0 / jnp.sum(total, axis=0, keepdims=True)
    delta = jnp.sum(delta, axis=0, keepdims=True) * inverse
    for n in range(WINDOW // TILE):
        part = slice(n * TILE, (n + 1) * TILE)
        probs = sb[part] * inverse
        grads = probs * (db[part] - delta)
        if n < EDGE:
            lower = lower_of(n)
            near = slice(WINDOW + n * TILE, WINDOW + (n + 1) * TILE)
            pb[near] = jnp.where(lower, probs, 0.0).astype(BF16)
            tb[near] = jnp.where(lower, grads, 0.0).astype(BF16)
            pb[part] = jnp.where(lower, 0.0, probs).astype(BF16)
            tb[part] = jnp.where(lower, 0.0, grads).astype(BF16)
        else:
            pb[part] = probs.astype(BF16)
            tb[part] = grads.astype(BF16)


def kernel(
    starts, q_ref, k_ref, v_ref, g_ref, dq_ref, dk_ref, dv_ref,
    qb, gb, kx, vx, kt, sb, db, sb2, db2, pb, tb, dka, dva, hs, hr, dqo, dko, dvo,
    in_recv, in_send, halo_recv, halo_send, back_recv, back_send, out_recv, out_send,
):
    ctx = lax.axis_index("ctx")
    place = lax.axis_index("fsdp")
    me = lax.rem(place, PEERS)
    half = place // PEERS
    block = ctx * 2 + half
    following = (lax.rem(ctx + half, BLOCKS // 2), (1 - half) * PEERS + me)
    previous = (lax.rem(ctx + half + BLOCKS // 2 - 1, BLOCKS // 2), (1 - half) * PEERS + me)

    def peer(j):
        x = lax.rem(me // 4 + j // 4, 4)
        y = lax.rem(lax.rem(me, 4) + lax.rem(j, 4), 4)
        return x * 4 + y

    def device(p):
        return (ctx, half * PEERS + p)

    barrier = pltpu.get_barrier_semaphore()

    def greet(j, carry):
        pl.semaphore_signal(barrier, inc=1, device_id=device(peer(j)), device_id_type=MESH)
        return carry

    lax.fori_loop(1, PEERS, greet, 0)

    for neighbour in (following, previous):
        pl.semaphore_signal(barrier, inc=1, device_id=neighbour, device_id_type=MESH)
    pl.semaphore_wait(barrier, PEERS + 1)

    def keys_of(ref, buf):
        def source(s, p):
            return ref.at[s, :, rows_of(p * HEAD, HEAD)]

        return source, lambda s: buf.at[s, pl.ds(WINDOW, OWN), :]

    def heads_of(ref, buf, h):
        def source(s, p):
            return ref.at[s, :, rows_of((2 * p + h) * HEAD, HEAD)]

        return source, lambda s: buf.at[s, h]

    incoming = {
        K: keys_of(k_ref, kx),
        V: keys_of(v_ref, vx),
        Q: heads_of(q_ref, qb, 0),
        G: heads_of(g_ref, gb, 0),
        Q + 2: heads_of(q_ref, qb, 1),
        G + 2: heads_of(g_ref, gb, 1),
    }

    def scatter(s, kind):
        source, buf = incoming[kind]
        landing = buf(s).at[rows_of(me * ROWS, ROWS), :]
        pltpu.make_async_copy(source(s, me), landing, in_recv.at[s, kind]).start()

        def send(j, carry):
            p = peer(j)
            pltpu.make_async_remote_copy(
                source(s, p), landing, in_send.at[s, kind], in_recv.at[s, kind],
                device_id=device(p), device_id_type=MESH,
            ).start()
            return carry

        lax.fori_loop(1, PEERS, send, 0)

    for s, kind in ARRIVALS:
        scatter(s, kind)

    dka[...] = jnp.zeros_like(dka)
    dva[...] = jnp.zeros_like(dva)

    def arrived(ref, sem):
        pltpu.make_async_copy(ref, ref, sem).wait()

    def turn(s, start):
        def one(t, carry):
            part = rows_of(start + t * TILE, TILE)
            kt[s, :, part] = kx[s, part, :].T
            return carry

        lax.fori_loop(0, OWN // TILE, one, 0)

    def forward(s):
        for kind, buf in ((K, kx), (V, vx)):
            own = buf.at[s, pl.ds(WINDOW, OWN), :]
            arrived(own, in_recv.at[s, kind])
            pltpu.make_async_remote_copy(
                own, buf.at[s, pl.ds(0, WINDOW), :], halo_send.at[s, kind], halo_recv.at[s, kind],
                device_id=following, device_id_type=MESH,
            ).start()

    def outgoing(s, kind, buf, columns):
        pltpu.make_async_copy(buf.at[rows_of(me * ROWS, ROWS), :], columns, out_recv.at[s, kind]).start()

        def send(j, carry):
            p = peer(j)
            pltpu.make_async_remote_copy(
                buf.at[rows_of(p * ROWS, ROWS), :], columns, out_send.at[s, kind], out_recv.at[s, kind],
                device_id=device(p), device_id_type=MESH,
            ).start()
            return carry

        lax.fori_loop(1, PEERS, send, 0)

    mine = rows_of(me * HEAD, HEAD)

    def finish(s):
        arrived(hr.at[s, 0], back_recv.at[s, 0])
        dko[s] = (dka[s, WINDOW:, :] * score_scale + hr[s, 0].astype(F32)).astype(BF16)
        outgoing(s, 2, dko.at[s], dk_ref.at[s, :, mine])
        arrived(hr.at[s, 1], back_recv.at[s, 1])
        dvo[s] = (dva[s, WINDOW:, :] + hr[s, 1].astype(F32)).astype(BF16)
        outgoing(s, 3, dvo.at[s], dv_ref.at[s, :, mine])

    scratch = ((sb, db), (sb2, db2))

    def unit(s, h):
        arrived(qb.at[s, h], in_recv.at[s, Q + 2 * h])
        arrived(gb.at[s, h], in_recv.at[s, G + 2 * h])
        q, g = qb.at[s, h], gb.at[s, h]
        scores(0, q, g, kx.at[s], vx.at[s], *scratch[0])
        for i in range(STEPS):
            here, span = spans(i)
            if i + 1 < STEPS:
                scores(i + 1, q, g, kx.at[s], vx.at[s], *scratch[(i + 1) % 2])
            score_grads(i, starts.at[s], block, *scratch[i % 2], pb, tb)
            dva[s, span, :] += dot(pb[...], g[here, :], NN)
            dka[s, span, :] += dot(tb[...], q[here, :], NN)
            if h == 1:
                hs[s, 0, here, :] = (dka[s, here, :] * score_scale).astype(BF16)
                hs[s, 1, here, :] = dva[s, here, :].astype(BF16)
            dqo[s, h, here, :] = (dot(kt[s, :, span], tb[...], NN) * score_scale).T.astype(BF16)
            if h == 1:
                for n in range(2):
                    pltpu.make_async_remote_copy(
                        hs.at[s, n, here, :], hr.at[s, n, here, :], back_send.at[s, n], back_recv.at[s, n],
                        device_id=previous, device_id_type=MESH,
                    ).start()
            if s > 0 and h == 1 and i == LATE:
                finish(s - 1)
        outgoing(s, h, dqo.at[s, h], dq_ref.at[s, :, rows_of((2 * me + h) * HEAD, HEAD)])

    for s in range(SEQS):
        forward(s)
        turn(s, WINDOW)
    for s in range(SEQS):
        for kind, buf in ((K, kx), (V, vx)):
            arrived(buf.at[s, pl.ds(0, WINDOW), :], halo_recv.at[s, kind])
        turn(s, 0)
        for h in range(2):
            unit(s, h)
    finish(SEQS - 1)

    others = pl.ds(0, OWN - ROWS)
    for s in range(SEQS):
        for h in range(2):
            arrived(dq_ref.at[s, :, pl.ds(0, PEERS * HEAD)], out_recv.at[s, h])
        arrived(dk_ref.at[s], out_recv.at[s, 2])
        arrived(dv_ref.at[s], out_recv.at[s, 3])
        for kind, buf in enumerate((dqo.at[s, 0], dqo.at[s, 1], dko.at[s], dvo.at[s])):
            arrived(buf.at[others, :], out_send.at[s, kind])
        for kind, (_, buf) in incoming.items():
            arrived(buf(s).at[others, :], in_send.at[s, kind])

        for kind, buf in ((K, kx), (V, vx)):
            arrived(buf.at[s, pl.ds(0, WINDOW), :], halo_send.at[s, kind])
        for n in range(2):
            arrived(hs.at[s, n], back_send.at[s, n])


def body(query, key, value, grad_out, tile_start):
    dma = pltpu.SemaphoreType.DMA
    hbm = pl.BlockSpec(memory_space=pl.ANY)
    grads = pl.pallas_call(
        kernel,
        out_shape=(
            pltpu.VMEM(query.shape, BF16),
            pltpu.VMEM(key.shape, BF16),
            pltpu.VMEM(value.shape, BF16),
        ),
        in_specs=[pl.BlockSpec(memory_space=pltpu.SMEM)] + [hbm] * 4,
        out_specs=[hbm] * 3,
        scratch_shapes=[
            pltpu.VMEM((SEQS, 2, OWN, HEAD), BF16),
            pltpu.VMEM((SEQS, 2, OWN, HEAD), BF16),
            pltpu.VMEM((SEQS, EXT, HEAD), BF16),
            pltpu.VMEM((SEQS, EXT, HEAD), BF16),
            pltpu.VMEM((SEQS, HEAD, EXT), BF16),
            pltpu.VMEM((SPAN, QUERIES), F32),
            pltpu.VMEM((SPAN, QUERIES), F32),
            pltpu.VMEM((SPAN, QUERIES), F32),
            pltpu.VMEM((SPAN, QUERIES), F32),
            pltpu.VMEM((SPAN, QUERIES), BF16),
            pltpu.VMEM((SPAN, QUERIES), BF16),
            pltpu.VMEM((SEQS, EXT, HEAD), F32),
            pltpu.VMEM((SEQS, EXT, HEAD), F32),
            pltpu.VMEM((SEQS, 2, WINDOW, HEAD), BF16),
            pltpu.VMEM((SEQS, 2, WINDOW, HEAD), BF16),
            pltpu.VMEM((SEQS, 2, OWN, HEAD), BF16),
            pltpu.VMEM((SEQS, OWN, HEAD), BF16),
            pltpu.VMEM((SEQS, OWN, HEAD), BF16),
            dma((SEQS, 6)), dma((SEQS, 6)),
            dma((SEQS, 2)), dma((SEQS, 2)),
            dma((SEQS, 2)), dma((SEQS, 2)),
            dma((SEQS, 4)), dma((SEQS, 4)),
        ],
        compiler_params=pltpu.CompilerParams(
            collective_id=0, has_side_effects=True, vmem_limit_bytes=64400000
        ),
        name="attention_grads",
    )(tile_start, query, key, value, grad_out)
    return placed(grads)


def place(dq_in, dk_in, dv_in, dq_out, dk_out, dv_out, left):
    copies = [
        pltpu.make_async_copy(ref, out, left.at[n])
        for n, (ref, out) in enumerate(((dq_in, dq_out), (dk_in, dk_out), (dv_in, dv_out)))
    ]
    for copy in copies:
        copy.start()
    for copy in copies:
        copy.wait()


def placed(grads):
    dma = pltpu.SemaphoreType.DMA
    hbm = pl.BlockSpec(memory_space=pl.ANY)
    return pl.pallas_call(
        place,
        out_shape=tuple(jax.ShapeDtypeStruct(g.shape, g.dtype) for g in grads),
        in_specs=[hbm] * 3,
        out_specs=[hbm] * 3,
        scratch_shapes=[dma((3,))],
        compiler_params=pltpu.CompilerParams(vmem_limit_bytes=2**20),
        name="place_grads",
    )(*grads)


def solution(mesh):
    spread = P(None, ("ctx", "fsdp"), None)
    return jax.shard_map(
        body, mesh=mesh, in_specs=(spread,) * 4 + (P(),), out_specs=(spread,) * 3, check_vma=False
    )
```

```python
import functools
import math

import jax
import jax.numpy as jnp
from jax import lax
from jax.experimental import pallas as pl
from jax.experimental.pallas import tpu as pltpu
from jax.sharding import PartitionSpec as P

MESH = pl.DeviceIdType.MESH
F32 = jnp.float32
BF16 = jnp.bfloat16

HEAD = 128
TILE = 128
WINDOW = 1024
SEQS = 2
PEERS = 16
OTHERS = (10, 9, 11, 6, 14, 8, 2, 5, 7, 13, 15, 1, 3, 4, 12)
BLOCKS = 8
OWN = 1024
ROWS = OWN // PEERS
TILES = OWN // TILE
QUERIES = 256
STEPS = OWN // QUERIES
LATE = 1
EDGE = QUERIES // TILE
SPAN = WINDOW + QUERIES
EXT = WINDOW + OWN
NEG = -1e30

score_scale = 168.0 ** (-0.5)
exp2_scale = score_scale * math.log2(math.e)

NT = (((1,), (1,)), ((), ()))
NN = (((1,), (0,)), ((), ()))

K, V, Q, G = range(4)
ARRIVALS = (
    [(s, kind) for s in range(SEQS) for kind in (K, V)]
    + [(s, kind + 2 * h) for s in range(SEQS) for h in range(2) for kind in (Q, G)]
)


def dot(a, b, dims):
    return lax.dot_general(a, b, dims, preferred_element_type=F32)


def rows_of(start, size):
    return pl.ds(pl.multiple_of(start, size), size)


def fold(x):
    return x.reshape(x.shape[0] // 8, 8, QUERIES)


def lower_of(n):
    row = lax.broadcasted_iota(jnp.int32, (TILE, QUERIES), 0) + n * TILE
    return row <= lax.broadcasted_iota(jnp.int32, (TILE, QUERIES), 1)


def spans(i):
    return pl.ds(i * QUERIES, QUERIES), pl.ds(i * QUERIES, SPAN)


def scores(i, q, g, keys, values, sb, db):
    here, span = spans(i)
    sb[...] = dot(keys[span, :], q[here, :], NT)
    db[...] = dot(values[span, :], g[here, :], NT)


def score_grads(i, starts, block, sb, db, pb, tb):
    lane = lax.broadcasted_iota(jnp.int32, (1, QUERIES), 1)
    tile = block * TILES + EDGE * i
    first = [starts[tile], starts[tile + 1]]
    bias = []
    for n in range(SPAN // TILE):
        key_tile = tile - WINDOW // TILE + n
        seen = [jnp.where(key_tile >= f, 0.0, NEG).astype(F32) for f in first]
        bias.append(jnp.where(lane < TILE, seen[0], seen[1]))
    top = None
    for n in range(WINDOW // TILE):
        part = slice(n * TILE, (n + 1) * TILE)
        if n < EDGE:
            lower = lower_of(n)
            near = slice(WINDOW + n * TILE, WINDOW + (n + 1) * TILE)
            merged = jnp.where(lower, sb[near] + bias[WINDOW // TILE + n], sb[part] + bias[n])
            sb[part] = merged
            db[part] = jnp.where(lower, db[near], db[part])
            high = jnp.max(fold(merged), axis=0)
        else:
            high = jnp.max(fold(sb[part]), axis=0) + bias[n]
        top = high if top is None else jnp.maximum(top, high)
    top = jnp.max(top, axis=0, keepdims=True) * exp2_scale
    total = jnp.zeros((8, QUERIES), F32)
    delta = jnp.zeros((8, QUERIES), F32)
    for n in range(WINDOW // TILE):
        part = slice(n * TILE, (n + 1) * TILE)
        weights = jnp.exp2(sb[part] * exp2_scale - (top if n < EDGE else top - bias[n]))
        total = total + jnp.sum(fold(weights), axis=0)
        delta = delta + jnp.sum(fold(weights * db[part]), axis=0)
        sb[part] = weights
    inverse = 1.0 / jnp.sum(total, axis=0, keepdims=True)
    delta = jnp.sum(delta, axis=0, keepdims=True) * inverse
    for n in range(WINDOW // TILE):
        part = slice(n * TILE, (n + 1) * TILE)
        probs = sb[part] * inverse
        grads = probs * (db[part] - delta)
        if n < EDGE:
            lower = lower_of(n)
            near = slice(WINDOW + n * TILE, WINDOW + (n + 1) * TILE)
            pb[near] = jnp.where(lower, probs, 0.0).astype(BF16)
            tb[near] = jnp.where(lower, grads, 0.0).astype(BF16)
            pb[part] = jnp.where(lower, 0.0, probs).astype(BF16)
            tb[part] = jnp.where(lower, 0.0, grads).astype(BF16)
        else:
            pb[part] = probs.astype(BF16)
            tb[part] = grads.astype(BF16)


def kernel(
    starts, q_ref, k_ref, v_ref, g_ref, dq_ref, dk_ref, dv_ref,
    qb, gb, kx, vx, kt, sb, db, sb2, db2, pb, tb, dka, dva, hs, hr, dqo, dko, dvo,
    in_recv, in_send, halo_recv, halo_send, back_recv, back_send, out_recv, out_send,
):
    ctx = lax.axis_index("ctx")
    place = lax.axis_index("fsdp")
    me = lax.rem(place, PEERS)
    half = place // PEERS
    block = ctx * 2 + half
    following = (lax.rem(ctx + half, BLOCKS // 2), (1 - half) * PEERS + me)
    previous = (lax.rem(ctx + half + BLOCKS // 2 - 1, BLOCKS // 2), (1 - half) * PEERS + me)

    def peer(j):
        x = lax.rem(me // 4 + j // 4, 4)
        y = lax.rem(lax.rem(me, 4) + j % 4, 4)
        return x * 4 + y

    def for_others(action):
        for j in OTHERS:
            action(j, 0)

    def device(p):
        return (ctx, half * PEERS + p)

    barrier = pltpu.get_barrier_semaphore()

    def greet(j, carry):
        pl.semaphore_signal(barrier, inc=1, device_id=device(peer(j)), device_id_type=MESH)
        return carry

    for_others(greet)

    for neighbour in (following, previous):
        pl.semaphore_signal(barrier, inc=1, device_id=neighbour, device_id_type=MESH)
    pl.semaphore_wait(barrier, PEERS + 1)

    def keys_of(ref, buf):
        def source(s, p):
            return ref.at[s, :, rows_of(p * HEAD, HEAD)]

        return source, lambda s: buf.at[s, pl.ds(WINDOW, OWN), :]

    def heads_of(ref, buf, h):
        def source(s, p):
            return ref.at[s, :, rows_of((2 * p + h) * HEAD, HEAD)]

        return source, lambda s: buf.at[s, h]

    incoming = {
        K: keys_of(k_ref, kx),
        V: keys_of(v_ref, vx),
        Q: heads_of(q_ref, qb, 0),
        G: heads_of(g_ref, gb, 0),
        Q + 2: heads_of(q_ref, qb, 1),
        G + 2: heads_of(g_ref, gb, 1),
    }

    def scatter(s, kind):
        source, buf = incoming[kind]
        landing = buf(s).at[rows_of(me * ROWS, ROWS), :]
        pltpu.make_async_copy(source(s, me), landing, in_recv.at[s, kind]).start()

        def send(j, carry):
            p = peer(j)
            pltpu.make_async_remote_copy(
                source(s, p), landing, in_send.at[s, kind], in_recv.at[s, kind],
                device_id=device(p), device_id_type=MESH,
            ).start()
            return carry

        for_others(send)

    for s, kind in ARRIVALS:
        scatter(s, kind)

    dka[...] = jnp.zeros_like(dka)
    dva[...] = jnp.zeros_like(dva)

    def arrived(ref, sem):
        pltpu.make_async_copy(ref, ref, sem).wait()

    def turn(s, start):
        def one(t, carry):
            part = rows_of(start + t * TILE, TILE)
            kt[s, :, part] = kx[s, part, :].T
            return carry

        lax.fori_loop(0, OWN // TILE, one, 0)

    def forward(s):
        for kind, buf in ((K, kx), (V, vx)):
            own = buf.at[s, pl.ds(WINDOW, OWN), :]
            arrived(own, in_recv.at[s, kind])
            pltpu.make_async_remote_copy(
                own, buf.at[s, pl.ds(0, WINDOW), :], halo_send.at[s, kind], halo_recv.at[s, kind],
                device_id=following, device_id_type=MESH,
            ).start()

    def outgoing(s, kind, buf, columns):
        pltpu.make_async_copy(buf.at[rows_of(me * ROWS, ROWS), :], columns, out_recv.at[s, kind]).start()

        def send(j, carry):
            p = peer(j)
            pltpu.make_async_remote_copy(
                buf.at[rows_of(p * ROWS, ROWS), :], columns, out_send.at[s, kind], out_recv.at[s, kind],
                device_id=device(p), device_id_type=MESH,
            ).start()
            return carry

        for_others(send)

    mine = rows_of(me * HEAD, HEAD)

    def finish(s):
        arrived(hr.at[s, 0], back_recv.at[s, 0])
        dko[s] = (dka[s, WINDOW:, :] * score_scale + hr[s, 0].astype(F32)).astype(BF16)
        outgoing(s, 2, dko.at[s], dk_ref.at[s, :, mine])
        arrived(hr.at[s, 1], back_recv.at[s, 1])
        dvo[s] = (dva[s, WINDOW:, :] + hr[s, 1].astype(F32)).astype(BF16)
        outgoing(s, 3, dvo.at[s], dv_ref.at[s, :, mine])

    scratch = ((sb, db), (sb2, db2))

    def unit(s, h):
        arrived(qb.at[s, h], in_recv.at[s, Q + 2 * h])
        arrived(gb.at[s, h], in_recv.at[s, G + 2 * h])
        q, g = qb.at[s, h], gb.at[s, h]
        scores(0, q, g, kx.at[s], vx.at[s], *scratch[0])
        for i in range(STEPS):
            here, span = spans(i)
            if i + 1 < STEPS:
                scores(i + 1, q, g, kx.at[s], vx.at[s], *scratch[(i + 1) % 2])
            score_grads(i, starts.at[s], block, *scratch[i % 2], pb, tb)
            dva[s, span, :] += dot(pb[...], g[here, :], NN)
            dka[s, span, :] += dot(tb[...], q[here, :], NN)
            if h == 1:
                hs[s, 0, here, :] = (dka[s, here, :] * score_scale).astype(BF16)
                hs[s, 1, here, :] = dva[s, here, :].astype(BF16)
            dqo[s, h, here, :] = (dot(kt[s, :, span], tb[...], NN) * score_scale).T.astype(BF16)
            if h == 1:
                for n in range(2):
                    pltpu.make_async_remote_copy(
                        hs.at[s, n, here, :], hr.at[s, n, here, :], back_send.at[s, n], back_recv.at[s, n],
                        device_id=previous, device_id_type=MESH,
                    ).start()
            if s > 0 and h == 1 and i == LATE:
                finish(s - 1)
        outgoing(s, h, dqo.at[s, h], dq_ref.at[s, :, rows_of((2 * me + h) * HEAD, HEAD)])

    for s in range(SEQS):
        forward(s)
        turn(s, WINDOW)
    for s in range(SEQS):
        for kind, buf in ((K, kx), (V, vx)):
            arrived(buf.at[s, pl.ds(0, WINDOW), :], halo_recv.at[s, kind])
        turn(s, 0)
        for h in range(2):
            unit(s, h)
    finish(SEQS - 1)

    others = pl.ds(0, OWN - ROWS)
    for s in range(SEQS):
        for h in range(2):
            arrived(dq_ref.at[s, :, pl.ds(0, PEERS * HEAD)], out_recv.at[s, h])
        arrived(dk_ref.at[s], out_recv.at[s, 2])
        arrived(dv_ref.at[s], out_recv.at[s, 3])
        for kind, buf in enumerate((dqo.at[s, 0], dqo.at[s, 1], dko.at[s], dvo.at[s])):
            arrived(buf.at[others, :], out_send.at[s, kind])
        for kind, (_, buf) in incoming.items():
            arrived(buf(s).at[others, :], in_send.at[s, kind])

        for kind, buf in ((K, kx), (V, vx)):
            arrived(buf.at[s, pl.ds(0, WINDOW), :], halo_send.at[s, kind])
        for n in range(2):
            arrived(hs.at[s, n], back_send.at[s, n])


def body(query, key, value, grad_out, tile_start):
    dma = pltpu.SemaphoreType.DMA
    hbm = pl.BlockSpec(memory_space=pl.ANY)
    grads = pl.pallas_call(
        kernel,
        out_shape=(
            pltpu.VMEM(query.shape, BF16),
            pltpu.VMEM(key.shape, BF16),
            pltpu.VMEM(value.shape, BF16),
        ),
        in_specs=[pl.BlockSpec(memory_space=pltpu.SMEM)] + [hbm] * 4,
        out_specs=[hbm] * 3,
        scratch_shapes=[
            pltpu.VMEM((SEQS, 2, OWN, HEAD), BF16),
            pltpu.VMEM((SEQS, 2, OWN, HEAD), BF16),
            pltpu.VMEM((SEQS, EXT, HEAD), BF16),
            pltpu.VMEM((SEQS, EXT, HEAD), BF16),
            pltpu.VMEM((SEQS, HEAD, EXT), BF16),
            pltpu.VMEM((SPAN, QUERIES), F32),
            pltpu.VMEM((SPAN, QUERIES), F32),
            pltpu.VMEM((SPAN, QUERIES), F32),
            pltpu.VMEM((SPAN, QUERIES), F32),
            pltpu.VMEM((SPAN, QUERIES), BF16),
            pltpu.VMEM((SPAN, QUERIES), BF16),
            pltpu.VMEM((SEQS, EXT, HEAD), F32),
            pltpu.VMEM((SEQS, EXT, HEAD), F32),
            pltpu.VMEM((SEQS, 2, WINDOW, HEAD), BF16),
            pltpu.VMEM((SEQS, 2, WINDOW, HEAD), BF16),
            pltpu.VMEM((SEQS, 2, OWN, HEAD), BF16),
            pltpu.VMEM((SEQS, OWN, HEAD), BF16),
            pltpu.VMEM((SEQS, OWN, HEAD), BF16),
            dma((SEQS, 6)), dma((SEQS, 6)),
            dma((SEQS, 2)), dma((SEQS, 2)),
            dma((SEQS, 2)), dma((SEQS, 2)),
            dma((SEQS, 4)), dma((SEQS, 4)),
        ],
        compiler_params=pltpu.CompilerParams(
            collective_id=0, has_side_effects=True, vmem_limit_bytes=64400000
        ),
        name="attention_grads",
    )(tile_start, query, key, value, grad_out)
    return placed(grads)


def place(dq_in, dk_in, dv_in, dq_out, dk_out, dv_out, left):
    copies = [
        pltpu.make_async_copy(ref, out, left.at[n])
        for n, (ref, out) in enumerate(((dq_in, dq_out), (dk_in, dk_out), (dv_in, dv_out)))
    ]
    for copy in copies:
        copy.start()
    for copy in copies:
        copy.wait()


def placed(grads):
    dma = pltpu.SemaphoreType.DMA
    hbm = pl.BlockSpec(memory_space=pl.ANY)
    return pl.pallas_call(
        place,
        out_shape=tuple(jax.ShapeDtypeStruct(g.shape, g.dtype) for g in grads),
        in_specs=[hbm] * 3,
        out_specs=[hbm] * 3,
        scratch_shapes=[dma((3,))],
        compiler_params=pltpu.CompilerParams(vmem_limit_bytes=2**20),
        name="place_grads",
    )(*grads)


def solution(mesh):
    spread = P(None, ("ctx", "fsdp"), None)
    return jax.shard_map(
        body, mesh=mesh, in_specs=(spread,) * 4 + (P(),), out_specs=(spread,) * 3, check_vma=False
    )
```

```python
import functools
import math

import jax
import jax.numpy as jnp
from jax import lax
from jax.experimental import pallas as pl
from jax.experimental.pallas import tpu as pltpu
from jax.sharding import PartitionSpec as P

MESH = pl.DeviceIdType.MESH
F32 = jnp.float32
BF16 = jnp.bfloat16

HEAD = 128
TILE = 128
WINDOW = 1024
SEQS = 2
PEERS = 16
OTHERS = (10, 9, 11, 6, 14, 8, 2, 5, 7, 13, 15, 1, 3, 4, 12)
BLOCKS = 8
OWN = 1024
ROWS = OWN // PEERS
TILES = OWN // TILE
QUERIES = 256
STEPS = OWN // QUERIES
LATE = 1
EDGE = QUERIES // TILE
SPAN = WINDOW + QUERIES
EXT = WINDOW + OWN
NEG = -1e30

score_scale = 168.0 ** (-0.5)
exp2_scale = score_scale * math.log2(math.e)

NT = (((1,), (1,)), ((), ()))
NN = (((1,), (0,)), ((), ()))

K, V, Q, G = range(4)
ARRIVALS = (
    [(s, kind) for s in range(SEQS) for kind in (K, V)]
    + [(s, kind + 2 * h) for s in range(SEQS) for h in range(2) for kind in (Q, G)]
)


def dot(a, b, dims):
    return lax.dot_general(a, b, dims, preferred_element_type=F32)


def rows_of(start, size):
    return pl.ds(pl.multiple_of(start, size), size)


def fold(x):
    return x.reshape(x.shape[0] // 8, 8, QUERIES)


def lower_of(n):
    row = lax.broadcasted_iota(jnp.int32, (TILE, QUERIES), 0) + n * TILE
    return row <= lax.broadcasted_iota(jnp.int32, (TILE, QUERIES), 1)


def spans(i):
    return pl.ds(i * QUERIES, QUERIES), pl.ds(i * QUERIES, SPAN)


def scores(i, q, g, keys, values, sb, db):
    here, span = spans(i)
    sb[...] = dot(keys[span, :], q[here, :], NT)
    db[...] = dot(values[span, :], g[here, :], NT)


def score_grads(i, starts, block, sb, db, pb, tb):
    lane = lax.broadcasted_iota(jnp.int32, (1, QUERIES), 1)
    tile = block * TILES + EDGE * i
    first = [starts[tile], starts[tile + 1]]
    bias = []
    for n in range(SPAN // TILE):
        key_tile = tile - WINDOW // TILE + n
        seen = [jnp.where(key_tile >= f, 0.0, NEG).astype(F32) for f in first]
        bias.append(jnp.where(lane < TILE, seen[0], seen[1]))
    top = None
    for n in range(WINDOW // TILE):
        part = slice(n * TILE, (n + 1) * TILE)
        if n < EDGE:
            lower = lower_of(n)
            near = slice(WINDOW + n * TILE, WINDOW + (n + 1) * TILE)
            merged = jnp.where(lower, sb[near] + bias[WINDOW // TILE + n], sb[part] + bias[n])
            sb[part] = merged
            db[part] = jnp.where(lower, db[near], db[part])
            high = jnp.max(fold(merged), axis=0)
        else:
            high = jnp.max(fold(sb[part]), axis=0) + bias[n]
        top = high if top is None else jnp.maximum(top, high)
    top = jnp.max(top, axis=0, keepdims=True) * exp2_scale
    total = jnp.zeros((8, QUERIES), F32)
    delta = jnp.zeros((8, QUERIES), F32)
    for n in range(WINDOW // TILE):
        part = slice(n * TILE, (n + 1) * TILE)
        weights = jnp.exp2(sb[part] * exp2_scale - (top if n < EDGE else top - bias[n]))
        total = total + jnp.sum(fold(weights), axis=0)
        delta = delta + jnp.sum(fold(weights * db[part]), axis=0)
        sb[part] = weights
    inverse = 1.0 / jnp.sum(total, axis=0, keepdims=True)
    delta = jnp.sum(delta, axis=0, keepdims=True) * inverse
    for n in range(WINDOW // TILE):
        part = slice(n * TILE, (n + 1) * TILE)
        probs = sb[part] * inverse
        grads = probs * (db[part] - delta)
        if n < EDGE:
            lower = lower_of(n)
            near = slice(WINDOW + n * TILE, WINDOW + (n + 1) * TILE)
            pb[near] = jnp.where(lower, probs, 0.0).astype(BF16)
            tb[near] = jnp.where(lower, grads, 0.0).astype(BF16)
            pb[part] = jnp.where(lower, 0.0, probs).astype(BF16)
            tb[part] = jnp.where(lower, 0.0, grads).astype(BF16)
        else:
            pb[part] = probs.astype(BF16)
            tb[part] = grads.astype(BF16)


def kernel(
    starts, q_ref, k_ref, v_ref, g_ref, dq_ref, dk_ref, dv_ref,
    qb, gb, kx, vx, kt, sb, db, sb2, db2, pb, tb, dka, dva, hs, hr, dqo, dko, dvo,
    in_recv, in_send, halo_recv, halo_send, back_recv, back_send, out_recv, out_send,
):
    ctx = lax.axis_index("ctx")
    place = lax.axis_index("fsdp")
    me = lax.rem(place, PEERS)
    half = place // PEERS
    block = ctx * 2 + half
    following = (lax.rem(ctx + half, BLOCKS // 2), (1 - half) * PEERS + me)
    previous = (lax.rem(ctx + half + BLOCKS // 2 - 1, BLOCKS // 2), (1 - half) * PEERS + me)

    def peer(j):
        x = lax.rem(me // 4 + j // 4, 4)
        y = lax.rem(lax.rem(me, 4) + j % 4, 4)
        return x * 4 + y

    def for_others(action):
        for j in OTHERS:
            action(j, 0)

    def device(p):
        return (ctx, half * PEERS + p)

    barrier = pltpu.get_barrier_semaphore()

    def greet(j, carry):
        pl.semaphore_signal(barrier, inc=1, device_id=device(peer(j)), device_id_type=MESH)
        return carry

    for_others(greet)

    for neighbour in (following, previous):
        pl.semaphore_signal(barrier, inc=1, device_id=neighbour, device_id_type=MESH)
    pl.semaphore_wait(barrier, PEERS + 1)

    def keys_of(ref, buf):
        def source(s, p):
            return ref.at[s, :, rows_of(p * HEAD, HEAD)]

        return source, lambda s: buf.at[s, pl.ds(WINDOW, OWN), :]

    def heads_of(ref, buf, h):
        def source(s, p):
            return ref.at[s, :, rows_of((2 * p + h) * HEAD, HEAD)]

        return source, lambda s: buf.at[s, h]

    incoming = {
        K: keys_of(k_ref, kx),
        V: keys_of(v_ref, vx),
        Q: heads_of(q_ref, qb, 0),
        G: heads_of(g_ref, gb, 0),
        Q + 2: heads_of(q_ref, qb, 1),
        G + 2: heads_of(g_ref, gb, 1),
    }

    def scatter(s, kind):
        source, buf = incoming[kind]
        landing = buf(s).at[rows_of(me * ROWS, ROWS), :]
        pltpu.make_async_copy(source(s, me), landing, in_recv.at[s, kind]).start()

        def send(j, carry):
            p = peer(j)
            pltpu.make_async_remote_copy(
                source(s, p), landing, in_send.at[s, kind], in_recv.at[s, kind],
                device_id=device(p), device_id_type=MESH,
            ).start()
            return carry

        for_others(send)

    for s, kind in ARRIVALS:
        scatter(s, kind)

    dka[...] = jnp.zeros_like(dka)
    dva[...] = jnp.zeros_like(dva)

    def arrived(ref, sem):
        pltpu.make_async_copy(ref, ref, sem).wait()

    def turn(s, start):
        def one(t, carry):
            part = rows_of(start + t * TILE, TILE)
            kt[s, :, part] = kx[s, part, :].T
            return carry

        lax.fori_loop(0, OWN // TILE, one, 0)

    def forward(s):
        for kind, buf in ((K, kx), (V, vx)):
            own = buf.at[s, pl.ds(WINDOW, OWN), :]
            arrived(own, in_recv.at[s, kind])
            pltpu.make_async_remote_copy(
                own, buf.at[s, pl.ds(0, WINDOW), :], halo_send.at[s, kind], halo_recv.at[s, kind],
                device_id=following, device_id_type=MESH,
            ).start()

    def outgoing(s, kind, buf, columns):
        pltpu.make_async_copy(buf.at[rows_of(me * ROWS, ROWS), :], columns, out_recv.at[s, kind]).start()

        def send(j, carry):
            p = peer(j)
            pltpu.make_async_remote_copy(
                buf.at[rows_of(p * ROWS, ROWS), :], columns, out_send.at[s, kind], out_recv.at[s, kind],
                device_id=device(p), device_id_type=MESH,
            ).start()
            return carry

        for_others(send)

    mine = rows_of(me * HEAD, HEAD)

    def finish(s):
        arrived(hr.at[s, 0], back_recv.at[s, 0])
        dko[s] = (dka[s, WINDOW:, :] * score_scale + hr[s, 0].astype(F32)).astype(BF16)
        arrived(hr.at[s, 1], back_recv.at[s, 1])
        dvo[s] = (dva[s, WINDOW:, :] + hr[s, 1].astype(F32)).astype(BF16)
        outgoing(s, 2, dko.at[s], dk_ref.at[s, :, mine])
        outgoing(s, 3, dvo.at[s], dv_ref.at[s, :, mine])

    scratch = ((sb, db), (sb2, db2))

    def unit(s, h):
        arrived(qb.at[s, h], in_recv.at[s, Q + 2 * h])
        arrived(gb.at[s, h], in_recv.at[s, G + 2 * h])
        q, g = qb.at[s, h], gb.at[s, h]
        scores(0, q, g, kx.at[s], vx.at[s], *scratch[0])
        for i in range(STEPS):
            here, span = spans(i)
            if i + 1 < STEPS:
                scores(i + 1, q, g, kx.at[s], vx.at[s], *scratch[(i + 1) % 2])
            score_grads(i, starts.at[s], block, *scratch[i % 2], pb, tb)
            dva[s, span, :] += dot(pb[...], g[here, :], NN)
            dka[s, span, :] += dot(tb[...], q[here, :], NN)
            if h == 1:
                hs[s, 0, here, :] = (dka[s, here, :] * score_scale).astype(BF16)
                hs[s, 1, here, :] = dva[s, here, :].astype(BF16)
            dqo[s, h, here, :] = (dot(kt[s, :, span], tb[...], NN) * score_scale).T.astype(BF16)
            if h == 1:
                for n in range(2):
                    pltpu.make_async_remote_copy(
                        hs.at[s, n, here, :], hr.at[s, n, here, :], back_send.at[s, n], back_recv.at[s, n],
                        device_id=previous, device_id_type=MESH,
                    ).start()
            if s > 0 and h == 1 and i == LATE:
                finish(s - 1)
        outgoing(s, h, dqo.at[s, h], dq_ref.at[s, :, rows_of((2 * me + h) * HEAD, HEAD)])

    for s in range(SEQS):
        forward(s)
        turn(s, WINDOW)
    for s in range(SEQS):
        for kind, buf in ((K, kx), (V, vx)):
            arrived(buf.at[s, pl.ds(0, WINDOW), :], halo_recv.at[s, kind])
        turn(s, 0)
        for h in range(2):
            unit(s, h)
    finish(SEQS - 1)

    others = pl.ds(0, OWN - ROWS)
    for s in range(SEQS):
        for h in range(2):
            arrived(dq_ref.at[s, :, pl.ds(0, PEERS * HEAD)], out_recv.at[s, h])
        arrived(dk_ref.at[s], out_recv.at[s, 2])
        arrived(dv_ref.at[s], out_recv.at[s, 3])
        for kind, buf in enumerate((dqo.at[s, 0], dqo.at[s, 1], dko.at[s], dvo.at[s])):
            arrived(buf.at[others, :], out_send.at[s, kind])
        for kind, (_, buf) in incoming.items():
            arrived(buf(s).at[others, :], in_send.at[s, kind])

        for kind, buf in ((K, kx), (V, vx)):
            arrived(buf.at[s, pl.ds(0, WINDOW), :], halo_send.at[s, kind])
        for n in range(2):
            arrived(hs.at[s, n], back_send.at[s, n])


def body(query, key, value, grad_out, tile_start):
    dma = pltpu.SemaphoreType.DMA
    hbm = pl.BlockSpec(memory_space=pl.ANY)
    grads = pl.pallas_call(
        kernel,
        out_shape=(
            pltpu.VMEM(query.shape, BF16),
            pltpu.VMEM(key.shape, BF16),
            pltpu.VMEM(value.shape, BF16),
        ),
        in_specs=[pl.BlockSpec(memory_space=pltpu.SMEM)] + [hbm] * 4,
        out_specs=[hbm] * 3,
        scratch_shapes=[
            pltpu.VMEM((SEQS, 2, OWN, HEAD), BF16),
            pltpu.VMEM((SEQS, 2, OWN, HEAD), BF16),
            pltpu.VMEM((SEQS, EXT, HEAD), BF16),
            pltpu.VMEM((SEQS, EXT, HEAD), BF16),
            pltpu.VMEM((SEQS, HEAD, EXT), BF16),
            pltpu.VMEM((SPAN, QUERIES), F32),
            pltpu.VMEM((SPAN, QUERIES), F32),
            pltpu.VMEM((SPAN, QUERIES), F32),
            pltpu.VMEM((SPAN, QUERIES), F32),
            pltpu.VMEM((SPAN, QUERIES), BF16),
            pltpu.VMEM((SPAN, QUERIES), BF16),
            pltpu.VMEM((SEQS, EXT, HEAD), F32),
            pltpu.VMEM((SEQS, EXT, HEAD), F32),
            pltpu.VMEM((SEQS, 2, WINDOW, HEAD), BF16),
            pltpu.VMEM((SEQS, 2, WINDOW, HEAD), BF16),
            pltpu.VMEM((SEQS, 2, OWN, HEAD), BF16),
            pltpu.VMEM((SEQS, OWN, HEAD), BF16),
            pltpu.VMEM((SEQS, OWN, HEAD), BF16),
            dma((SEQS, 6)), dma((SEQS, 6)),
            dma((SEQS, 2)), dma((SEQS, 2)),
            dma((SEQS, 2)), dma((SEQS, 2)),
            dma((SEQS, 4)), dma((SEQS, 4)),
        ],
        compiler_params=pltpu.CompilerParams(
            collective_id=0, has_side_effects=True, vmem_limit_bytes=64400000
        ),
        name="attention_grads",
    )(tile_start, query, key, value, grad_out)
    return placed(grads)


def place(dq_in, dk_in, dv_in, dq_out, dk_out, dv_out, left):
    copies = [
        pltpu.make_async_copy(ref, out, left.at[n])
        for n, (ref, out) in enumerate(((dq_in, dq_out), (dk_in, dk_out), (dv_in, dv_out)))
    ]
    for copy in copies:
        copy.start()
    for copy in copies:
        copy.wait()


def placed(grads):
    dma = pltpu.SemaphoreType.DMA
    hbm = pl.BlockSpec(memory_space=pl.ANY)
    return pl.pallas_call(
        place,
        out_shape=tuple(jax.ShapeDtypeStruct(g.shape, g.dtype) for g in grads),
        in_specs=[hbm] * 3,
        out_specs=[hbm] * 3,
        scratch_shapes=[dma((3,))],
        compiler_params=pltpu.CompilerParams(vmem_limit_bytes=2**20),
        name="place_grads",
    )(*grads)


def solution(mesh):
    spread = P(None, ("ctx", "fsdp"), None)
    return jax.shard_map(
        body, mesh=mesh, in_specs=(spread,) * 4 + (P(),), out_specs=(spread,) * 3, check_vma=False
    )
```
